256 devices in a mesh: chain: 64 (over y, x, z_hi, core), sector: 4 (over z_lo).
Axes of the slice: x: 4, y: 4, z: 8 (z_hi: 2, z_lo: 4; z = z_hi * 4 + z_lo), core: 2. Of those that a mesh axis runs over, the one named last changes fastest.
Arguments:
- psi: float32 [64, 16, 256, 256], P('chain', 'sector'), may hold values from -6 to 6
- kept_rank: int32 [64, 16], P('chain', 'sector'), may hold values from 64 to 256, as said below
- step_size: float32 [64, 3], P('chain'), may hold values from 0.2 to 0.6
- left_env: bfloat16 [64, 2, 16, 256, 256], P('chain', None, 'sector'), may hold values from -0.375 to 0.375
- right_env: bfloat16 [64, 2, 16, 256, 256], P('chain', None, 'sector'), may hold values from -0.375 to 0.375
- hop_left: bfloat16 [64, 2, 16, 256, 256], P('chain', None, 'sector'), may hold values from -0.375 to 0.375
- hop_right: bfloat16 [64, 2, 16, 256, 256], P('chain', None, 'sector'), may hold values from -0.375 to 0.375
- hop_source: int32 [2, 16], replicated, may hold values from 0 to 15, each once within a row
Outputs:
- site_state: float32 [64, 16, 256, 256], P('chain', 'sector')
- merged_left: float32 [64, 2, 16, 256, 256], P('chain', None, 'sector')
- merged_right: float32 [64, 2, 16, 256, 256], P('chain', None, 'sector')
The draws below stay inside these ranges and needn't reach their ends.
Inputs may be any that keep to these rules, and one draw needn't show every extreme that they name: `kept_rank`: each partition has one sector whose kept rank is the full 256.
All inputs are finite; a program needn't handle non-finite values.
Results may differ from the reference program's by a relative error of at most 0.009.
Values may be sent and summed in bfloat16 or wider, within the bound.
A program may use at most 64 MiB of HBM per device.

```python
import jax
import jax.numpy as jnp
from jax import lax

BLK = 256
TERMS = 2
HOPS = 2
STEPS = 3
SECT = 16
CHI = 4096
PARTS_SIZE = 64


def draw_kept_rank(key, part):
    first_key = jax.random.fold_in(key, 11)
    second_key = jax.random.fold_in(key, 23)
    ranks = jax.random.randint(first_key, (PARTS_SIZE, SECT), BLK // 4, BLK + 1)
    chosen = jax.random.randint(second_key, (PARTS_SIZE,), 0, SECT)
    column = lax.broadcasted_iota(jnp.int32, (PARTS_SIZE, SECT), 1)
    return jnp.where(column == chosen[:, None], BLK, ranks).astype(jnp.int32)


def block_levels(rng, shape, cuts, low, largest):
    gain = 1.0
    for axis_at, shards_of in cuts:
        steps = jax.random.uniform(jax.random.fold_in(jax.random.fold_in(rng, 6), axis_at), (shards_of,), jnp.float32, low / len(cuts), largest / len(cuts))
        gain = gain * jnp.repeat(jnp.exp(steps), shape[axis_at] // shards_of).reshape((-1,) + (1,) * (len(shape) - 1 - axis_at))
    return gain


def centred(rng, dims, scale, bound, split=(), held_as=jnp.bfloat16):
    factor_of = block_levels(rng, dims, split, -0.22, 0.18) if split else 1.0
    result = jax.random.normal(rng, dims, jnp.float32) * scale * factor_of
    return jnp.minimum(jnp.maximum(result, -bound), bound).astype(held_as)


def setup_inputs(seed: int = 0) -> dict:
    key_list = jax.random.split(jax.random.key(seed), 9)
    return {
        "psi": centred(key_list[0], (PARTS_SIZE, SECT, BLK, BLK), 1.0, 6.0, ((0, 64), (1, 4)), jnp.float32),
        "kept_rank": draw_kept_rank(jax.random.fold_in(key_list[8], 71), 0),
        "step_size": jnp.clip(0.2 + 0.400000021 * jax.random.uniform(key_list[2], (PARTS_SIZE, STEPS), jnp.float32) ** block_levels(key_list[2], (PARTS_SIZE, STEPS), ((0, 64),), -0.2, 0.2), 0.2, 0.6),
        "left_env": centred(key_list[3], (PARTS_SIZE, TERMS, SECT, BLK, BLK), BLK ** -0.5, 0.375, ((0, 64), (2, 4))),
        "right_env": centred(key_list[4], (PARTS_SIZE, TERMS, SECT, BLK, BLK), BLK ** -0.5, 0.375, ((0, 64), (2, 4))),
        "hop_left": centred(key_list[5], (PARTS_SIZE, HOPS, SECT, BLK, BLK), BLK ** -0.5, 0.375, ((0, 64), (2, 4))),
        "hop_right": centred(key_list[6], (PARTS_SIZE, HOPS, SECT, BLK, BLK), BLK ** -0.5, 0.375, ((0, 64), (2, 4))),
        "hop_source": jax.vmap(lambda own: jax.random.permutation(own, SECT))(jax.random.split(key_list[7], HOPS)).reshape((HOPS, SECT)).astype(jnp.int32),
    }


def apply_operator(state, left_env, right_env, hop_left, hop_right, hop_source, mask):
    f32 = jnp.float32
    state_b = state.astype(jnp.bfloat16)
    inner = jnp.einsum('atij,tjk->atik', left_env.astype(f32), state_b.astype(f32)).astype(jnp.bfloat16)
    image = jnp.einsum('atik,atkl->til', inner.astype(f32), right_env.astype(f32))
    picked = state_b[hop_source]
    hop_inner = jnp.einsum('btij,btjk->btik', hop_left.astype(f32), picked.astype(f32)).astype(jnp.bfloat16)
    image = image + jnp.einsum('btik,btkl->til', hop_inner.astype(f32), hop_right.astype(f32))
    return image * mask

def reference(psi, kept_rank, step_size, left_env, right_env, hop_left, hop_right, hop_source):
    f32 = jnp.float32

    def one_part(items):
        block, ranks, steps, left_one, right_one, hop_a, hop_b = items
        row_index = lax.broadcasted_iota(jnp.int32, (SECT, BLK), 1)
        kept_rows = (row_index < ranks[:, None]).astype(f32)
        mask = kept_rows[:, :, None] * kept_rows[:, None, :]
        state = block * mask
        for step in range(STEPS):
            image = apply_operator(state, left_one, right_one, hop_a, hop_b, hop_source, mask)
            self_dot = jnp.sum(state * state)
            cross = jnp.sum(state * image)
            quotient = cross / self_dot
            state = state - steps[step] * (image - quotient * state)
            state = state / jnp.sqrt(jnp.sum(state * state))
        final_b = state.astype(jnp.bfloat16).astype(f32)
        left_half = jnp.einsum('tji,atjk->atik', final_b, left_one.astype(f32)).astype(jnp.bfloat16)
        left_new = CHI * jnp.einsum('atik,tkl->atil', left_half.astype(f32), final_b)
        right_half = jnp.einsum('atij,tkj->atik', right_one.astype(f32), final_b).astype(jnp.bfloat16)
        right_new = CHI * jnp.einsum('tij,atjk->atik', final_b, right_half.astype(f32))
        return (state, left_new, right_new)
    site_state, left_new, right_new = lax.map(one_part, (psi, kept_rank, step_size, left_env, right_env, hop_left, hop_right))
    zeros_one = jnp.zeros((1, TERMS, SECT, BLK, BLK), f32)
    merged_left = left_env.astype(f32) + jnp.concatenate([zeros_one, left_new[:-1]], axis=0)
    merged_right = right_env.astype(f32) + jnp.concatenate([right_new[1:], zeros_one], axis=0)
    return (site_state, merged_left, merged_right)
```

```python
import jax
import jax.numpy as jnp
from jax import lax
from jax.experimental import pallas as pl
from jax.experimental.pallas import tpu as pltpu
from jax.sharding import PartitionSpec as P

MESH = pl.DeviceIdType.MESH
STEPS = 3
OWN = 4
SLOTS = 8
CHUNKS = 4
ENTRIES = tuple((i, j) for j in range(STEPS + 1) for i in range(j + 1))


def entry(i, j):
    return ENTRIES.index((min(i, j), max(i, j)))


def pair_dot(a, b):
    rows, cols = a.shape
    return jnp.sum((a * b).reshape(rows // 8, 8, cols), axis=0)


def quadratic(coef, other, gram, row_shift, col_shift):
    total = None
    for i, a in enumerate(coef):
        for j, b in enumerate(other):
            term = a * b * gram[entry(i + row_shift, j + col_shift)]
            total = term if total is None else total + term
    return total


def kernel(
    rank, step_size, source,
    psi_hbm, left_hbm, right_hbm, hop_left_hbm, hop_right_hbm,
    state_out, from_left, from_right,
    *scratch,
):
    f32, bf16 = jnp.float32, jnp.bfloat16
    chunk_bufs = [scratch[k * CHUNKS : (k + 1) * CHUNKS] for k in range(STEPS)]
    at = STEPS * CHUNKS
    packed = scratch[at : at + STEPS]
    at += STEPS
    vec = scratch[at : at + STEPS + 1]
    at += STEPS + 1
    (psi, left, right, hop_left, hop_right, final, send_left, send_right, gram_acc, gram_in, gram_out,
     load_sem, send_sem, recv_sem, gram_send, gram_recv, merge_send, merge_recv, out_sem) = scratch[at:]

    me_c = lax.axis_index("chain")
    n_c = lax.axis_size("chain")
    z = lax.axis_index("sector")
    near = z + 1 - 2 * lax.rem(z, 2)
    peer = 3 - z
    far = 3 - near
    inner_far = jnp.where(z == 0, 2, 1)
    is_inner = jnp.logical_or(z == 1, z == 2)
    is_outer = jnp.logical_not(is_inner)
    nxt = lax.rem(me_c + 1, n_c)
    prv = lax.rem(me_c + n_c - 1, n_c)
    blk = psi.shape[1]
    rows = blk // CHUNKS
    chi = float(16 * blk)

    loads = [
        pltpu.make_async_copy(psi_hbm.at[0], psi, load_sem.at[0]),
        pltpu.make_async_copy(left_hbm.at[0], left, load_sem.at[1]),
        pltpu.make_async_copy(right_hbm.at[0], right, load_sem.at[2]),
        pltpu.make_async_copy(hop_left_hbm.at[0], hop_left, load_sem.at[3]),
        pltpu.make_async_copy(hop_right_hbm.at[0], hop_right, load_sem.at[4]),
    ]
    for copy in loads:
        copy.start()

    barrier = pltpu.get_barrier_semaphore()
    for d in range(1, 4):
        pl.semaphore_signal(barrier, inc=1, device_id=(me_c, lax.rem(z + d, 4)), device_id_type=MESH)
    for c in (prv, nxt):
        pl.semaphore_signal(barrier, inc=1, device_id=(c, z), device_id_type=MESH)

    row_at = lax.broadcasted_iota(jnp.int32, (blk, blk), 0)
    col_at = lax.broadcasted_iota(jnp.int32, (blk, blk), 1)

    def kept(j, value):
        r = rank[0, j]
        return jnp.where((row_at < r) & (col_at < r), value, 0.0)

    def put_own(k, j, value):
        value = value.astype(bf16)
        for c in range(CHUNKS):
            chunk_bufs[k][c][12 + j] = value[c * rows : (c + 1) * rows]

    def block(k, i):
        return jnp.concatenate([chunk_bufs[k][c][i] for c in range(CHUNKS)], axis=0)

    def remote(src, dst, k, c, kind, to):
        return pltpu.make_async_remote_copy(
            src_ref=src, dst_ref=dst, send_sem=send_sem.at[k, c, kind], recv_sem=recv_sem.at[k, c, kind],
            device_id=(me_c, to), device_id_type=MESH,
        )

    def to_peer(k, c):
        buf = chunk_bufs[k][c]
        return remote(buf.at[12:16], buf.at[0:4], k, c, 0, peer)

    def to_far(k, c):
        buf = chunk_bufs[k][c]
        return remote(buf.at[12:16], buf.at[4:8], k, c, 1, inner_far)

    def to_near(k, c):
        buf = chunk_bufs[k][c]
        return remote(buf.at[12:16], buf.at[8:12], k, c, 2, near)

    def to_outer(k, c):
        return remote(packed[k].at[c], chunk_bufs[k][c].at[0:SLOTS], k, c, 3, near)

    def send_own(k):
        @pl.when(is_outer)
        def _():
            for c in range(CHUNKS):
                to_far(k, c).start()
                to_near(k, c).start()

        @pl.when(is_inner)
        def _():
            for c in range(CHUNKS):
                to_peer(k, c).start()

    def owner_of(s):
        owner = s // OWN
        return owner, s - owner * OWN

    def exchange(k):
        @pl.when(is_inner)
        def _():
            picks = []
            for b in range(2):
                for j in range(OWN):
                    owner, loc = owner_of(source[b, near * OWN + j])
                    picks.append(
                        jnp.where(owner == peer, loc, jnp.where(owner == far, 4 + loc, 12 + loc))
                    )
            for c in range(CHUNKS):
                to_peer(k, c).wait_recv()
                to_far(k, c).wait_recv()
                to_near(k, c).wait_recv()
                for s, pick in enumerate(picks):
                    packed[k][c, s] = chunk_bufs[k][c][pick]
                to_outer(k, c).start()

        @pl.when(is_outer)
        def _():
            for c in range(CHUNKS):
                to_outer(k, c).wait_recv()

    def picked(b, j):
        owner, loc = owner_of(source[b, z * OWN + j])
        at_inner = jnp.where(
            owner == peer, loc, jnp.where(owner == far, 4 + loc, jnp.where(owner == near, 8 + loc, 12 + loc))
        )
        at_outer = jnp.where(owner == z, 12 + loc, b * OWN + j)
        return jnp.where(is_inner, at_inner, at_outer)

    def dot(a, b):
        return jnp.dot(a, b, preferred_element_type=f32)

    gram_acc[...] = jnp.zeros_like(gram_acc)
    loads[0].wait()

    def first(j, carry):
        value = kept(j, psi[j])
        vec[0][j] = value
        put_own(0, j, value)
        gram_acc[entry(0, 0)] += pair_dot(value, value)
        return carry

    lax.fori_loop(0, OWN, first, 0)
    pl.semaphore_wait(barrier, 5)
    send_own(0)
    for copy in loads[1:]:
        copy.wait()

    for k in range(STEPS):

        def on_site(j, carry):
            own = block(k, 12 + j)
            total = None
            for a in range(2):
                half = dot(left[a, j], own).astype(bf16)
                term = dot(half, right[a, j])
                total = term if total is None else total + term
            vec[k + 1][j] = total
            return carry

        lax.fori_loop(0, OWN, on_site, 0)
        exchange(k)

        def hop(j, carry):
            total = vec[k + 1][j]
            for b in range(2):
                half = dot(hop_left[b, j], block(k, picked(b, j))).astype(bf16)
                total = total + dot(half, hop_right[b, j])
            total = kept(j, total)
            vec[k + 1][j] = total
            if k + 1 < STEPS:
                put_own(k + 1, j, total)
            for i in range(k + 2):
                other = total if i == k + 1 else vec[i][j]
                gram_acc[entry(i, k + 1)] += pair_dot(total, other)
            return carry

        lax.fori_loop(0, OWN, hop, 0)
        if k + 1 < STEPS:
            send_own(k + 1)

    for e in range(len(ENTRIES)):
        line = jnp.sum(gram_acc[e], axis=0, keepdims=True)
        gram_out[e : e + 1, :] = line[:, :128] + line[:, 128:]
    gram_out[len(ENTRIES) :, :] = jnp.zeros((16 - len(ENTRIES), 128), f32)

    def gram_copy(d):
        return pltpu.make_async_remote_copy(
            src_ref=gram_out, dst_ref=gram_in.at[d - 1], send_sem=gram_send.at[d - 1],
            recv_sem=gram_recv.at[d - 1], device_id=(me_c, lax.rem(z + d, 4)), device_id_type=MESH,
        )

    for d in range(1, 4):
        gram_copy(d).start()
    for d in range(1, 4):
        gram_copy(d).wait_recv()
    gram_all = jnp.sum(gram_out[...] + gram_in[0] + gram_in[1] + gram_in[2], axis=1, keepdims=True)
    gram = [gram_all[e : e + 1] for e in range(len(ENTRIES))]

    coef = [jnp.ones((1, 1), f32)]
    for k in range(STEPS):
        h = step_size[0, k]
        self_dot = quadratic(coef, coef, gram, 0, 0)
        cross = quadratic(coef, coef, gram, 0, 1)
        grow = 1.0 + h * (cross / self_dot)
        new = [grow * c for c in coef] + [jnp.zeros((1, 1), f32)]
        for i, c in enumerate(coef):
            new[i + 1] = new[i + 1] - h * c
        scale = 1.0 / jnp.sqrt(quadratic(new, new, gram, 0, 0))
        coef = [c * scale for c in new]

    def merge(direction, a, j):
        src, dst, to = ((send_left, from_left, nxt), (send_right, from_right, prv))[direction]
        return pltpu.make_async_remote_copy(
            src_ref=src.at[a, j], dst_ref=dst.at[a, j], send_sem=merge_send.at[direction, a, j],
            recv_sem=merge_recv.at[direction, a, j], device_id=(to, z), device_id_type=MESH,
        )

    has_next = me_c < n_c - 1
    has_prev = me_c > 0

    def finish(j, carry):
        value = coef[0] * vec[0][j]
        for i in range(1, STEPS + 1):
            value = value + coef[i] * vec[i][j]
        final[j] = value
        own = value.astype(bf16)
        own_t = value.T.astype(bf16)
        for a in range(2):
            half = dot(own_t, left[a, j]).astype(bf16)
            send_left[a, j] = (chi * dot(half, own)).astype(bf16)
            half = dot(right[a, j], own_t).astype(bf16)
            send_right[a, j] = (chi * dot(own, half)).astype(bf16)

        @pl.when(has_next)
        def _():
            for a in range(2):
                merge(0, a, j).start()

        @pl.when(has_prev)
        def _():
            for a in range(2):
                merge(1, a, j).start()

        return carry

    lax.fori_loop(0, OWN, finish, 0)
    put_state = pltpu.make_async_copy(final, state_out.at[0], out_sem)
    put_state.start()

    for k in range(STEPS):

        @pl.when(is_outer)
        def _():
            for c in range(CHUNKS):
                to_far(k, c).wait_send()
                to_near(k, c).wait_send()

        @pl.when(is_inner)
        def _():
            for c in range(CHUNKS):
                to_peer(k, c).wait_send()
                to_outer(k, c).wait_send()

    for d in range(1, 4):
        gram_copy(d).wait_send()

    @pl.when(has_next)
    def _():
        for a in range(2):
            for j in range(OWN):
                merge(0, a, j).wait_send()
                merge(1, a, j).wait_recv()

    @pl.when(has_prev)
    def _():
        for a in range(2):
            for j in range(OWN):
                merge(1, a, j).wait_send()
                merge(0, a, j).wait_recv()

    put_state.wait()


def on_device(psi, kept_rank, step_size, left_env, right_env, hop_left, hop_right, hop_source):
    f32, bf16 = jnp.float32, jnp.bfloat16
    own, blk = psi.shape[1], psi.shape[2]
    rows = blk // CHUNKS
    env = (2, own, blk, blk)
    smem = pl.BlockSpec(memory_space=pltpu.SMEM)
    hbm = pl.BlockSpec(memory_space=pl.ANY)
    dma = pltpu.SemaphoreType.DMA
    state, from_left, from_right = pl.pallas_call(
        kernel,
        out_shape=(
            jax.ShapeDtypeStruct(psi.shape, f32),
            jax.ShapeDtypeStruct(env, bf16),
            jax.ShapeDtypeStruct(env, bf16),
        ),
        in_specs=[smem] * 3 + [hbm] * 5,
        out_specs=(hbm, hbm, hbm),
        scratch_shapes=[
            *[pltpu.VMEM((16, rows, blk), bf16) for _ in range(STEPS * CHUNKS)],
            *[pltpu.VMEM((CHUNKS, SLOTS, rows, blk), bf16) for _ in range(STEPS)],
            *[pltpu.VMEM((own, blk, blk), f32) for _ in range(STEPS + 1)],
            pltpu.VMEM((own, blk, blk), f32),
            *[pltpu.VMEM(env, bf16) for _ in range(4)],
            pltpu.VMEM((own, blk, blk), f32),
            pltpu.VMEM(env, bf16),
            pltpu.VMEM(env, bf16),
            pltpu.VMEM((len(ENTRIES), 8, blk), f32),
            pltpu.VMEM((3, 16, 128), f32),
            pltpu.VMEM((16, 128), f32),
            dma((5,)),
            dma((STEPS, CHUNKS, 4)),
            dma((STEPS, CHUNKS, 4)),
            dma((3,)),
            dma((3,)),
            dma((2, 2, own)),
            dma((2, 2, own)),
            dma,
        ],
        compiler_params=pltpu.CompilerParams(
            collective_id=0, has_side_effects=True, vmem_limit_bytes=48 * 1024 * 1024
        ),
    )(kept_rank, step_size, hop_source, psi, left_env, right_env, hop_left, hop_right)
    me_c = lax.axis_index("chain")
    last = lax.axis_size("chain") - 1
    merged_left = left_env[0].astype(f32) + jnp.where(me_c == 0, 0.0, from_left.astype(f32))
    merged_right = right_env[0].astype(f32) + jnp.where(me_c == last, 0.0, from_right.astype(f32))
    return state, merged_left[None], merged_right[None]


def solution(mesh):
    part = P("chain", "sector", None, None)
    term = P("chain", None, "sector", None, None)
    return jax.shard_map(
        on_device,
        mesh=mesh,
        in_specs=(part, P("chain", "sector"), P("chain", None), term, term, term, term, P()),
        out_specs=(part, term, term),
        check_vma=False,
    )
```

```python
import jax
import jax.numpy as jnp
from jax import lax
from jax.experimental import pallas as pl
from jax.experimental.pallas import tpu as pltpu
from jax.sharding import PartitionSpec as P

MESH = pl.DeviceIdType.MESH
STEPS = 3
OWN = 4
HOPS = 2
EARLY = 4
CHUNKS = 8
RELAY_LAG = CHUNKS - 2
LATE_LAG = 2
ENTRIES = tuple((i, j) for j in range(STEPS + 1) for i in range(j + 1))


def entry(i, j):
    return ENTRIES.index((min(i, j), max(i, j)))


def pair_dot(a, b):
    rows, cols = a.shape
    return jnp.sum((a * b).reshape(rows // 8, 8, cols), axis=0)


def quadratic(coef, other, gram, row_shift, col_shift):
    total = None
    for i, a in enumerate(coef):
        for j, b in enumerate(other):
            term = a * b * gram[entry(i + row_shift, j + col_shift)]
            total = term if total is None else total + term
    return total


def kernel(
    rank, step_size, source,
    psi_hbm, left_hbm, right_hbm, hop_left_hbm, hop_right_hbm,
    state_out, from_left, from_right,
    *scratch,
):
    f32, bf16 = jnp.float32, jnp.bfloat16
    per = STEPS * CHUNKS
    near_bufs = [scratch[k * CHUNKS : (k + 1) * CHUNKS] for k in range(STEPS)]
    far_bufs = [scratch[per + k * CHUNKS : per + (k + 1) * CHUNKS] for k in range(STEPS)]
    at = 2 * per
    early_bufs = scratch[at : at + STEPS]
    late_bufs = scratch[at + STEPS : at + 2 * STEPS]
    at += 2 * STEPS
    vec = scratch[at : at + STEPS + 1]
    at += STEPS + 1
    (psi, left, right, hop_left, hop_right, final, send_left, send_right, gram_acc, gram_in, gram_out, picks,
     load_sem, send_sem, recv_sem, gram_send, gram_recv, merge_send, merge_recv, out_sem) = scratch[at:]

    me_c = lax.axis_index("chain")
    n_c = lax.axis_size("chain")
    z = lax.axis_index("sector")
    near = z + 1 - 2 * lax.rem(z, 2)
    peer = 3 - z
    far = 3 - near
    is_inner = jnp.logical_or(z == 1, z == 2)
    is_outer = jnp.logical_not(is_inner)
    nxt = lax.rem(me_c + 1, n_c)
    prv = lax.rem(me_c + n_c - 1, n_c)
    blk = psi.shape[1]
    rows = blk // CHUNKS
    chi = float(16 * blk)

    loads = [
        pltpu.make_async_copy(psi_hbm.at[0], psi, load_sem.at[0]),
        pltpu.make_async_copy(left_hbm.at[0], left, load_sem.at[1]),
        pltpu.make_async_copy(right_hbm.at[0], right, load_sem.at[2]),
        pltpu.make_async_copy(hop_left_hbm.at[0], hop_left, load_sem.at[3]),
        pltpu.make_async_copy(hop_right_hbm.at[0], hop_right, load_sem.at[4]),
    ]
    for copy in loads:
        copy.start()

    barrier = pltpu.get_barrier_semaphore()
    for d in range(1, 4):
        pl.semaphore_signal(barrier, inc=1, device_id=(me_c, lax.rem(z + d, 4)), device_id_type=MESH)
    for c in (prv, nxt):
        pl.semaphore_signal(barrier, inc=1, device_id=(c, z), device_id_type=MESH)

    row_at = lax.broadcasted_iota(jnp.int32, (blk, blk), 0)
    col_at = lax.broadcasted_iota(jnp.int32, (blk, blk), 1)

    def kept(j, value):
        r = rank[0, j]
        return jnp.where((row_at < r) & (col_at < r), value, 0.0)

    def put_own(k, j, value):
        value = value.astype(bf16)
        for c in range(CHUNKS):
            near_bufs[k][c][4 + j] = value[c * rows : (c + 1) * rows]

    def own_block(k, j):
        return jnp.concatenate([near_bufs[k][c][4 + j] for c in range(CHUNKS)], axis=0)

    def chunk_of(k, c, i):
        return jnp.where(
            i < 8, near_bufs[k][c][jnp.minimum(i, 7)], far_bufs[k][c][jnp.maximum(i - 8, 0)]
        )

    def remote(src, dst, k, c, sent, received, to):
        return pltpu.make_async_remote_copy(
            src_ref=src, dst_ref=dst, send_sem=send_sem.at[k, c, sent], recv_sem=recv_sem.at[k, c, received],
            device_id=(me_c, to), device_id_type=MESH,
        )

    def to_peer(k, c):
        return remote(near_bufs[k][c].at[4:8], near_bufs[k][c].at[0:4], k, c, 0, 0, peer)

    def to_near(k, c):
        return remote(near_bufs[k][c].at[4:8], far_bufs[k][c].at[4:8], k, c, 0, 2, near)

    def relay(k, c):
        return remote(far_bufs[k][c].at[4:8], far_bufs[k][c].at[0:4], k, c, 1, 1, peer)

    def early(k, c):
        return remote(early_bufs[k].at[c], near_bufs[k][c].at[0:4], k, c, 2, 0, near)

    def late(k, c):
        return remote(late_bufs[k].at[c], far_bufs[k][c].at[0:4], k, c, 3, 1, near)

    def send_own(k):
        @pl.when(is_outer)
        def _():
            for c in range(CHUNKS):
                to_near(k, c).start()

        @pl.when(is_inner)
        def _():
            for c in range(CHUNKS):
                to_peer(k, c).start()

    def owner_of(s):
        owner = s // OWN
        return owner, s - owner * OWN

    outer = jnp.where(is_inner, near, z)
    zero, one = jnp.int32(0), jnp.int32(1)
    middle_seen = zero
    needed = [zero] * OWN
    entries = []
    for n in range(HOPS * OWN):
        owner, loc = owner_of(source[n // OWN, outer * OWN + n % OWN])
        is_far = owner == 3 - outer
        is_middle = jnp.logical_not(jnp.logical_or(is_far, owner == outer))
        entries.append((owner, loc, is_far, is_middle, middle_seen))
        middle_seen = middle_seen + jnp.where(is_middle, one, zero)
        for l in range(OWN):
            needed[l] = jnp.where(jnp.logical_and(is_far, loc == l), one, needed[l])
    free_rank = []
    seen = zero
    for l in range(OWN):
        free_rank.append(jnp.where(needed[l] == 0, seen, jnp.int32(-1)))
        seen = seen + (one - needed[l])
    for n, (owner, loc, is_far, is_middle, rank_n) in enumerate(entries):
        slot = zero
        for l in range(OWN):
            slot = jnp.where(free_rank[l] == rank_n - EARLY, jnp.int32(l), slot)
        row = jnp.where(is_middle, jnp.where(rank_n < EARLY, rank_n, 8 + slot), jnp.where(is_far, 8 + loc, 4 + loc))
        owner_z, loc_z = owner_of(source[n // OWN, z * OWN + n % OWN])
        at_inner = jnp.where(
            owner_z == z, 4 + loc_z, jnp.where(owner_z == peer, loc_z, jnp.where(owner_z == near, 12 + loc_z, 8 + loc_z))
        )
        picks[n] = jnp.where(is_inner, at_inner, row)
    for e in range(2 * EARLY):
        pick = zero if e < EARLY else jnp.where(needed[e - EARLY] == 1, jnp.int32(8 + e - EARLY), zero)
        for owner, loc, is_far, is_middle, rank_n in entries:
            mine = rank_n == e if e < EARLY else rank_n - EARLY == free_rank[e - EARLY]
            mine = jnp.logical_and(mine, is_middle)
            if e >= EARLY:
                mine = jnp.logical_and(mine, needed[e - EARLY] == 0)
            pick = jnp.where(mine, jnp.where(owner == z, 4 + loc, loc), pick)
        picks[HOPS * OWN + e] = pick

    def exchange(k, meanwhile):
        for i in range(CHUNKS + RELAY_LAG + LATE_LAG):

            @pl.when(is_inner)
            def _():
                if i < CHUNKS:
                    to_peer(k, i).wait_recv()
                    for e in range(EARLY):
                        early_bufs[k][i, e] = near_bufs[k][i][picks[HOPS * OWN + e]]
                    early(k, i).start()
                c = i - RELAY_LAG
                if 0 <= c < CHUNKS:
                    to_near(k, c).wait_recv()
                    relay(k, c).start()
                c -= LATE_LAG
                if c >= 0:
                    relay(k, c).wait_recv()
                    for e in range(EARLY):
                        late_bufs[k][c, e] = chunk_of(k, c, picks[HOPS * OWN + EARLY + e])
                    late(k, c).start()

            if i < OWN:
                meanwhile(i)

        @pl.when(is_outer)
        def _():
            for c in range(CHUNKS):
                early(k, c).wait_recv()
                late(k, c).wait_recv()

    def picked(k, b, j):
        i = picks[b * OWN + j]
        return jnp.concatenate([chunk_of(k, c, i) for c in range(CHUNKS)], axis=0)

    def dot(a, b):
        return jnp.dot(a, b, preferred_element_type=f32)

    gram_acc[...] = jnp.zeros_like(gram_acc)
    loads[0].wait()

    def first(j, carry):
        value = kept(j, psi[j])
        vec[0][j] = value
        put_own(0, j, value)
        gram_acc[entry(0, 0)] += pair_dot(value, value)
        return carry

    lax.fori_loop(0, OWN, first, 0, unroll=True)
    pl.semaphore_wait(barrier, 5)
    send_own(0)
    for copy in loads[1:]:
        copy.wait()

    for k in range(STEPS):

        def on_site(j):
            half = dot(left[:, j].reshape(2 * blk, blk), own_block(k, j)).astype(bf16)
            both = jnp.concatenate([half[:blk], half[blk:]], axis=1)
            vec[k + 1][j] = dot(both, right[:, j].reshape(2 * blk, blk))

        exchange(k, on_site)

        def hop(j, carry):
            both = jnp.concatenate(
                [dot(hop_left[b, j], picked(k, b, j)).astype(bf16) for b in range(HOPS)], axis=1
            )
            total = vec[k + 1][j] + dot(both, hop_right[:, j].reshape(2 * blk, blk))
            total = kept(j, total)
            vec[k + 1][j] = total
            if k + 1 < STEPS:
                put_own(k + 1, j, total)
            for i in range(k + 2):
                other = total if i == k + 1 else vec[i][j]
                gram_acc[entry(i, k + 1)] += pair_dot(total, other)
            return carry

        lax.fori_loop(0, OWN, hop, 0, unroll=True)
        if k + 1 < STEPS:
            send_own(k + 1)

    for e in range(len(ENTRIES)):
        line = jnp.sum(gram_acc[e], axis=0, keepdims=True)
        gram_out[e : e + 1, :] = line[:, :128] + line[:, 128:]
    gram_out[len(ENTRIES) :, :] = jnp.zeros((16 - len(ENTRIES), 128), f32)

    def gram_copy(d):
        return pltpu.make_async_remote_copy(
            src_ref=gram_out, dst_ref=gram_in.at[d - 1], send_sem=gram_send.at[d - 1],
            recv_sem=gram_recv.at[d - 1], device_id=(me_c, lax.rem(z + d, 4)), device_id_type=MESH,
        )

    for d in range(1, 4):
        gram_copy(d).start()
    for d in range(1, 4):
        gram_copy(d).wait_recv()
    gram_all = jnp.sum(gram_out[...] + gram_in[0] + gram_in[1] + gram_in[2], axis=1, keepdims=True)
    gram = [gram_all[e : e + 1] for e in range(len(ENTRIES))]

    coef = [jnp.ones((1, 1), f32)]
    for k in range(STEPS):
        h = step_size[0, k]
        self_dot = quadratic(coef, coef, gram, 0, 0)
        cross = quadratic(coef, coef, gram, 0, 1)
        grow = 1.0 + h * (cross / self_dot)
        new = [grow * c for c in coef] + [jnp.zeros((1, 1), f32)]
        for i, c in enumerate(coef):
            new[i + 1] = new[i + 1] - h * c
        scale = 1.0 / jnp.sqrt(quadratic(new, new, gram, 0, 0))
        coef = [c * scale for c in new]

    def merge(direction, a, j):
        src, dst, to = ((send_left, from_left, nxt), (send_right, from_right, prv))[direction]
        return pltpu.make_async_remote_copy(
            src_ref=src.at[a, j], dst_ref=dst.at[a, j], send_sem=merge_send.at[direction, a, j],
            recv_sem=merge_recv.at[direction, a, j], device_id=(to, z), device_id_type=MESH,
        )

    has_next = me_c < n_c - 1
    has_prev = me_c > 0

    def finish(j, carry):
        value = coef[0] * vec[0][j]
        for i in range(1, STEPS + 1):
            value = value + coef[i] * vec[i][j]
        final[j] = value
        own = value.astype(bf16)
        own_t = value.T.astype(bf16)
        for a in range(2):
            half = dot(own_t, left[a, j]).astype(bf16)
            send_left[a, j] = (chi * dot(half, own)).astype(bf16)
            half = dot(right[a, j], own_t).astype(bf16)
            send_right[a, j] = (chi * dot(own, half)).astype(bf16)

        @pl.when(has_next)
        def _():
            for a in range(2):
                merge(0, a, j).start()

        @pl.when(has_prev)
        def _():
            for a in range(2):
                merge(1, a, j).start()

        return carry

    lax.fori_loop(0, OWN, finish, 0, unroll=True)
    put_state = pltpu.make_async_copy(final, state_out.at[0], out_sem)
    put_state.start()

    for k in range(STEPS):

        @pl.when(is_outer)
        def _():
            for c in range(CHUNKS):
                to_near(k, c).wait_send()

        @pl.when(is_inner)
        def _():
            for c in range(CHUNKS):
                to_peer(k, c).wait_send()
                relay(k, c).wait_send()
                early(k, c).wait_send()
                late(k, c).wait_send()

    for d in range(1, 4):
        gram_copy(d).wait_send()

    @pl.when(has_next)
    def _():
        for a in range(2):
            for j in range(OWN):
                merge(0, a, j).wait_send()
                merge(1, a, j).wait_recv()

    @pl.when(has_prev)
    def _():
        for a in range(2):
            for j in range(OWN):
                merge(1, a, j).wait_send()
                merge(0, a, j).wait_recv()

    put_state.wait()


def on_device(psi, kept_rank, step_size, left_env, right_env, hop_left, hop_right, hop_source):
    f32, bf16 = jnp.float32, jnp.bfloat16
    own, blk = psi.shape[1], psi.shape[2]
    rows = blk // CHUNKS
    env = (2, own, blk, blk)
    smem = pl.BlockSpec(memory_space=pltpu.SMEM)
    hbm = pl.BlockSpec(memory_space=pl.ANY)
    dma = pltpu.SemaphoreType.DMA
    state, from_left, from_right = pl.pallas_call(
        kernel,
        out_shape=(
            jax.ShapeDtypeStruct(psi.shape, f32),
            jax.ShapeDtypeStruct(env, bf16),
            jax.ShapeDtypeStruct(env, bf16),
        ),
        in_specs=[smem] * 3 + [hbm] * 5,
        out_specs=(hbm, hbm, hbm),
        scratch_shapes=[
            *[pltpu.VMEM((8, rows, blk), bf16) for _ in range(2 * STEPS * CHUNKS)],
            *[pltpu.VMEM((CHUNKS, EARLY, rows, blk), bf16) for _ in range(2 * STEPS)],
            *[pltpu.VMEM((own, blk, blk), f32) for _ in range(STEPS + 1)],
            pltpu.VMEM((own, blk, blk), f32),
            *[pltpu.VMEM(env, bf16) for _ in range(4)],
            pltpu.VMEM((own, blk, blk), f32),
            pltpu.VMEM(env, bf16),
            pltpu.VMEM(env, bf16),
            pltpu.VMEM((len(ENTRIES), 8, blk), f32),
            pltpu.VMEM((3, 16, 128), f32),
            pltpu.VMEM((16, 128), f32),
            pltpu.SMEM((HOPS * OWN + 2 * EARLY,), jnp.int32),
            dma((5,)),
            dma((STEPS, CHUNKS, 4)),
            dma((STEPS, CHUNKS, 3)),
            dma((3,)),
            dma((3,)),
            dma((2, 2, own)),
            dma((2, 2, own)),
            dma,
        ],
        compiler_params=pltpu.CompilerParams(
            collective_id=0, has_side_effects=True, vmem_limit_bytes=67_000_000
        ),
    )(kept_rank, step_size, hop_source, psi, left_env, right_env, hop_left, hop_right)
    me_c = lax.axis_index("chain")
    last = lax.axis_size("chain") - 1
    merged_left = left_env[0].astype(f32) + jnp.where(me_c == 0, 0.0, from_left.astype(f32))
    merged_right = right_env[0].astype(f32) + jnp.where(me_c == last, 0.0, from_right.astype(f32))
    return state, merged_left[None], merged_right[None]


def solution(mesh):
    part = P("chain", "sector", None, None)
    term = P("chain", None, "sector", None, None)
    return jax.shard_map(
        on_device,
        mesh=mesh,
        in_specs=(part, P("chain", "sector"), P("chain", None), term, term, term, term, P()),
        out_specs=(part, term, term),
        check_vma=False,
    )
```

```python
import jax
import jax.numpy as jnp
from jax import lax
from jax.experimental import pallas as pl
from jax.experimental.pallas import tpu as pltpu
from jax.sharding import PartitionSpec as P

MESH = pl.DeviceIdType.MESH
STEPS = 3
OWN = 4
HOPS = 2
EARLY = 4
CHUNKS = 8
RELAY_LAG = CHUNKS - 2
LATE_LAG = 2
ENTRIES = tuple((i, j) for j in range(STEPS + 1) for i in range(j + 1))


def entry(i, j):
    return ENTRIES.index((min(i, j), max(i, j)))


def pair_dot(a, b):
    rows, cols = a.shape
    return jnp.sum((a * b).reshape(rows // 8, 8, cols), axis=0)


def quadratic(coef, other, gram, row_shift, col_shift):
    total = None
    for i, a in enumerate(coef):
        for j, b in enumerate(other):
            term = a * b * gram[entry(i + row_shift, j + col_shift)]
            total = term if total is None else total + term
    return total


def kernel(
    rank, step_size, source,
    psi_hbm, left_hbm, right_hbm, hop_left_hbm, hop_right_hbm,
    final, merged_left, merged_right,
    *scratch,
):
    f32, bf16 = jnp.float32, jnp.bfloat16
    per = STEPS * CHUNKS
    near_bufs = [scratch[k * CHUNKS : (k + 1) * CHUNKS] for k in range(STEPS)]
    far_bufs = [scratch[per + k * CHUNKS : per + (k + 1) * CHUNKS] for k in range(STEPS)]
    at = 2 * per
    early_bufs = scratch[at : at + STEPS]
    late_bufs = scratch[at + STEPS : at + 2 * STEPS]
    at += 2 * STEPS
    vec = scratch[at : at + STEPS + 1]
    at += STEPS + 1
    (psi, left, right, hop_left, hop_right, send_left, send_right, from_left, from_right, gram_acc, gram_in, gram_out, picks,
     load_sem, send_sem, recv_sem, gram_send, gram_recv, merge_send, merge_recv) = scratch[at:]

    me_c = lax.axis_index("chain")
    n_c = lax.axis_size("chain")
    z = lax.axis_index("sector")
    near = z + 1 - 2 * lax.rem(z, 2)
    peer = 3 - z
    far = 3 - near
    is_inner = jnp.logical_or(z == 1, z == 2)
    is_outer = jnp.logical_not(is_inner)
    nxt = lax.rem(me_c + 1, n_c)
    prv = lax.rem(me_c + n_c - 1, n_c)
    blk = psi.shape[1]
    rows = blk // CHUNKS
    chi = float(16 * blk)

    loads = [
        pltpu.make_async_copy(psi_hbm.at[0], psi, load_sem.at[0]),
        pltpu.make_async_copy(left_hbm.at[0], left, load_sem.at[1]),
        pltpu.make_async_copy(right_hbm.at[0], right, load_sem.at[2]),
        pltpu.make_async_copy(hop_left_hbm.at[0], hop_left, load_sem.at[3]),
        pltpu.make_async_copy(hop_right_hbm.at[0], hop_right, load_sem.at[4]),
    ]
    for copy in loads:
        copy.start()

    barrier = pltpu.get_barrier_semaphore()
    for d in range(1, 4):
        pl.semaphore_signal(barrier, inc=1, device_id=(me_c, lax.rem(z + d, 4)), device_id_type=MESH)
    has_next = me_c < n_c - 1
    has_prev = me_c > 0

    @pl.when(has_prev)
    def _():
        pl.semaphore_signal(barrier, inc=1, device_id=(prv, z), device_id_type=MESH)

    @pl.when(has_next)
    def _():
        pl.semaphore_signal(barrier, inc=1, device_id=(nxt, z), device_id_type=MESH)


    row_at = lax.broadcasted_iota(jnp.int32, (blk, blk), 0)
    col_at = lax.broadcasted_iota(jnp.int32, (blk, blk), 1)

    def kept(j, value):
        r = rank[0, j]
        return jnp.where((row_at < r) & (col_at < r), value, 0.0)

    def put_own(k, j, value):
        value = value.astype(bf16)
        for c in range(CHUNKS):
            near_bufs[k][c][4 + j] = value[c * rows : (c + 1) * rows]

    def own_block(k, j):
        return jnp.concatenate([near_bufs[k][c][4 + j] for c in range(CHUNKS)], axis=0)

    def chunk_of(k, c, i):
        return jnp.where(
            i < 8, near_bufs[k][c][jnp.minimum(i, 7)], far_bufs[k][c][jnp.maximum(i - 8, 0)]
        )

    def remote(src, dst, k, c, sent, received, to):
        return pltpu.make_async_remote_copy(
            src_ref=src, dst_ref=dst, send_sem=send_sem.at[k, c, sent], recv_sem=recv_sem.at[k, c, received],
            device_id=(me_c, to), device_id_type=MESH,
        )

    def to_peer(k, c):
        return remote(near_bufs[k][c].at[4:8], near_bufs[k][c].at[0:4], k, c, 0, 0, peer)

    def to_near(k, c):
        return remote(near_bufs[k][c].at[4:8], far_bufs[k][c].at[4:8], k, c, 0, 2, near)

    def relay(k, c):
        return remote(far_bufs[k][c].at[4:8], far_bufs[k][c].at[0:4], k, c, 1, 1, peer)

    def early(k, c):
        return remote(early_bufs[k].at[c], near_bufs[k][c].at[0:4], k, c, 2, 0, near)

    def late(k, c):
        return remote(late_bufs[k].at[c], far_bufs[k][c].at[0:4], k, c, 3, 1, near)

    def send_own(k):
        @pl.when(is_outer)
        def _():
            for c in range(CHUNKS):
                to_near(k, c).start()

        @pl.when(is_inner)
        def _():
            for c in range(CHUNKS):
                to_peer(k, c).start()

    def owner_of(s):
        owner = s // OWN
        return owner, s - owner * OWN

    outer = jnp.where(is_inner, near, z)
    zero, one = jnp.int32(0), jnp.int32(1)
    middle_seen = zero
    needed = [zero] * OWN
    entries = []
    for n in range(HOPS * OWN):
        owner, loc = owner_of(source[n // OWN, outer * OWN + n % OWN])
        is_far = owner == 3 - outer
        is_middle = jnp.logical_not(jnp.logical_or(is_far, owner == outer))
        entries.append((owner, loc, is_far, is_middle, middle_seen))
        middle_seen = middle_seen + jnp.where(is_middle, one, zero)
        for l in range(OWN):
            needed[l] = jnp.where(jnp.logical_and(is_far, loc == l), one, needed[l])
    free_rank = []
    seen = zero
    for l in range(OWN):
        free_rank.append(jnp.where(needed[l] == 0, seen, jnp.int32(-1)))
        seen = seen + (one - needed[l])
    for n, (owner, loc, is_far, is_middle, rank_n) in enumerate(entries):
        slot = zero
        for l in range(OWN):
            slot = jnp.where(free_rank[l] == rank_n - EARLY, jnp.int32(l), slot)
        row = jnp.where(is_middle, jnp.where(rank_n < EARLY, rank_n, 8 + slot), jnp.where(is_far, 8 + loc, 4 + loc))
        owner_z, loc_z = owner_of(source[n // OWN, z * OWN + n % OWN])
        at_inner = jnp.where(
            owner_z == z, 4 + loc_z, jnp.where(owner_z == peer, loc_z, jnp.where(owner_z == near, 12 + loc_z, 8 + loc_z))
        )
        picks[n] = jnp.where(is_inner, at_inner, row)
    for e in range(2 * EARLY):
        pick = zero if e < EARLY else jnp.where(needed[e - EARLY] == 1, jnp.int32(8 + e - EARLY), zero)
        for owner, loc, is_far, is_middle, rank_n in entries:
            mine = rank_n == e if e < EARLY else rank_n - EARLY == free_rank[e - EARLY]
            mine = jnp.logical_and(mine, is_middle)
            if e >= EARLY:
                mine = jnp.logical_and(mine, needed[e - EARLY] == 0)
            pick = jnp.where(mine, jnp.where(owner == z, 4 + loc, loc), pick)
        picks[HOPS * OWN + e] = pick

    def exchange(k, meanwhile):
        for i in range(CHUNKS + RELAY_LAG + LATE_LAG):

            @pl.when(is_inner)
            def _():
                if i < CHUNKS:
                    to_peer(k, i).wait_recv()
                    for e in range(EARLY):
                        early_bufs[k][i, e] = near_bufs[k][i][picks[HOPS * OWN + e]]
                    early(k, i).start()
                c = i - RELAY_LAG
                if 0 <= c < CHUNKS:
                    to_near(k, c).wait_recv()
                    relay(k, c).start()
                c -= LATE_LAG
                if c >= 0:
                    relay(k, c).wait_recv()
                    for e in range(EARLY):
                        late_bufs[k][c, e] = chunk_of(k, c, picks[HOPS * OWN + EARLY + e])
                    late(k, c).start()

            if i < OWN:
                meanwhile(i)

        @pl.when(is_outer)
        def _():
            for c in range(CHUNKS):
                early(k, c).wait_recv()
                late(k, c).wait_recv()

    def picked(k, b, j):
        i = picks[b * OWN + j]
        return jnp.concatenate([chunk_of(k, c, i) for c in range(CHUNKS)], axis=0)

    def dot(a, b):
        return jnp.dot(a, b, preferred_element_type=f32)

    gram_acc[...] = jnp.zeros_like(gram_acc)
    loads[0].wait()

    def first(j, carry):
        value = kept(j, psi[j])
        vec[0][j] = value
        put_own(0, j, value)
        gram_acc[entry(0, 0)] += pair_dot(value, value)
        return carry

    lax.fori_loop(0, OWN, first, 0, unroll=True)
    pl.semaphore_wait(barrier, jnp.where(jnp.logical_and(has_prev, has_next), 5, 4))
    send_own(0)
    for copy in loads[1:]:
        copy.wait()

    for k in range(STEPS):

        def on_site(j):
            half = dot(left[:, j].reshape(2 * blk, blk), own_block(k, j)).astype(bf16)
            both = jnp.concatenate([half[:blk], half[blk:]], axis=1)
            vec[k + 1][j] = dot(both, right[:, j].reshape(2 * blk, blk))

        exchange(k, on_site)

        def hop(j, carry):
            both = jnp.concatenate(
                [dot(hop_left[b, j], picked(k, b, j)).astype(bf16) for b in range(HOPS)], axis=1
            )
            total = vec[k + 1][j] + dot(both, hop_right[:, j].reshape(2 * blk, blk))
            total = kept(j, total)
            vec[k + 1][j] = total
            if k + 1 < STEPS:
                put_own(k + 1, j, total)
            for i in range(k + 2):
                other = total if i == k + 1 else vec[i][j]
                gram_acc[entry(i, k + 1)] += pair_dot(total, other)
            return carry

        lax.fori_loop(0, OWN, hop, 0, unroll=True)
        if k + 1 < STEPS:
            send_own(k + 1)

    for e in range(len(ENTRIES)):
        line = jnp.sum(gram_acc[e], axis=0, keepdims=True)
        gram_out[e : e + 1, :] = line[:, :128] + line[:, 128:]
    gram_out[len(ENTRIES) :, :] = jnp.zeros((16 - len(ENTRIES), 128), f32)

    def gram_copy(d):
        return pltpu.make_async_remote_copy(
            src_ref=gram_out, dst_ref=gram_in.at[d - 1], send_sem=gram_send.at[d - 1],
            recv_sem=gram_recv.at[d - 1], device_id=(me_c, lax.rem(z + d, 4)), device_id_type=MESH,
        )

    for d in range(1, 4):
        gram_copy(d).start()
    for d in range(1, 4):
        gram_copy(d).wait_recv()
    gram_all = jnp.sum(gram_out[...] + gram_in[0] + gram_in[1] + gram_in[2], axis=1, keepdims=True)
    gram = [gram_all[e : e + 1] for e in range(len(ENTRIES))]

    coef = [jnp.ones((1, 1), f32)]
    for k in range(STEPS):
        h = step_size[0, k]
        self_dot = quadratic(coef, coef, gram, 0, 0)
        cross = quadratic(coef, coef, gram, 0, 1)
        grow = 1.0 + h * (cross / self_dot)
        new = [grow * c for c in coef] + [jnp.zeros((1, 1), f32)]
        for i, c in enumerate(coef):
            new[i + 1] = new[i + 1] - h * c
        scale = 1.0 / jnp.sqrt(quadratic(new, new, gram, 0, 0))
        coef = [c * scale for c in new]

    def merge(direction, a, j):
        src, dst, to = ((send_left, from_left, nxt), (send_right, from_right, prv))[direction]
        return pltpu.make_async_remote_copy(
            src_ref=src.at[a, j], dst_ref=dst.at[a, j], send_sem=merge_send.at[direction, a, j],
            recv_sem=merge_recv.at[direction, a, j], device_id=(to, z), device_id_type=MESH,
        )

    def finish(j, carry):
        value = coef[0] * vec[0][j]
        for i in range(1, STEPS + 1):
            value = value + coef[i] * vec[i][j]
        final[0, j] = value
        own = value.astype(bf16)
        own_t = value.T.astype(bf16)
        for a in range(2):
            half = dot(own_t, left[a, j]).astype(bf16)
            send_left[a, j] = (chi * dot(half, own)).astype(bf16)
            half = dot(right[a, j], own_t).astype(bf16)
            send_right[a, j] = (chi * dot(own, half)).astype(bf16)

        @pl.when(has_next)
        def _():
            for a in range(2):
                merge(0, a, j).start()

        @pl.when(has_prev)
        def _():
            for a in range(2):
                merge(1, a, j).start()

        return carry

    lax.fori_loop(0, OWN, finish, 0, unroll=True)
    def receive(direction, a, j, out, env, got):
        merge(direction, a, j).wait_recv()
        out[0, a, j] = env[a, j].astype(f32) + got[a, j].astype(f32)

    @pl.when(has_prev)
    def _():
        for j in range(OWN):
            for a in range(2):
                receive(0, a, j, merged_left, left, from_left)

    @pl.when(has_next)
    def _():
        for j in range(OWN):
            for a in range(2):
                receive(1, a, j, merged_right, right, from_right)

    @pl.when(jnp.logical_not(has_prev))
    def _():
        merged_left[0] = left[...].astype(f32)

    @pl.when(jnp.logical_not(has_next))
    def _():
        merged_right[0] = right[...].astype(f32)

    for k in range(STEPS):

        @pl.when(is_outer)
        def _():
            for c in range(CHUNKS):
                to_near(k, c).wait_send()

        @pl.when(is_inner)
        def _():
            for c in range(CHUNKS):
                to_peer(k, c).wait_send()
                relay(k, c).wait_send()
                early(k, c).wait_send()
                late(k, c).wait_send()

    for d in range(1, 4):
        gram_copy(d).wait_send()

    @pl.when(has_next)
    def _():
        for a in range(2):
            for j in range(OWN):
                merge(0, a, j).wait_send()

    @pl.when(has_prev)
    def _():
        for a in range(2):
            for j in range(OWN):
                merge(1, a, j).wait_send()


def write_out(*refs):
    count = (len(refs) - 1) // 2
    copies = [
        pltpu.make_async_copy(refs[i].at[0, j], refs[count + i].at[0, j], refs[-1].at[i, j])
        for i in range(count)
        for j in range(refs[i].shape[1])
    ]
    for copy in copies:
        copy.start()
    for copy in copies:
        copy.wait()


def on_device(psi, kept_rank, step_size, left_env, right_env, hop_left, hop_right, hop_source):
    f32, bf16 = jnp.float32, jnp.bfloat16
    own, blk = psi.shape[1], psi.shape[2]
    rows = blk // CHUNKS
    env = (2, own, blk, blk)
    smem = pl.BlockSpec(memory_space=pltpu.SMEM)
    hbm = pl.BlockSpec(memory_space=pl.ANY)
    dma = pltpu.SemaphoreType.DMA
    shapes = (psi.shape, left_env.shape, right_env.shape)
    held = [pltpu.with_memory_space_constraint(x, pltpu.HBM) for x in (psi, left_env, right_env, hop_left, hop_right)]
    results = pl.pallas_call(
        kernel,
        out_shape=tuple(pltpu.VMEM(shape, f32) for shape in shapes),
        in_specs=[smem] * 3 + [hbm] * 5,
        out_specs=(pl.BlockSpec(memory_space=pltpu.VMEM),) * 3,
        scratch_shapes=[
            *[pltpu.VMEM((8, rows, blk), bf16) for _ in range(2 * STEPS * CHUNKS)],
            *[pltpu.VMEM((CHUNKS, EARLY, rows, blk), bf16) for _ in range(2 * STEPS)],
            *[pltpu.VMEM((own, blk, blk), f32) for _ in range(STEPS + 1)],
            pltpu.VMEM((own, blk, blk), f32),
            *[pltpu.VMEM(env, bf16) for _ in range(4)],
            *[pltpu.VMEM(env, bf16) for _ in range(4)],
            pltpu.VMEM((len(ENTRIES), 8, blk), f32),
            pltpu.VMEM((3, 16, 128), f32),
            pltpu.VMEM((16, 128), f32),
            pltpu.SMEM((HOPS * OWN + 2 * EARLY,), jnp.int32),
            dma((5,)),
            dma((STEPS, CHUNKS, 4)),
            dma((STEPS, CHUNKS, 3)),
            dma((3,)),
            dma((3,)),
            dma((2, 2, own)),
            dma((2, 2, own)),
        ],
        compiler_params=pltpu.CompilerParams(
            collective_id=0, has_side_effects=True, vmem_limit_bytes=61_700_000
        ),
    )(kept_rank, step_size, hop_source, *held)
    return pl.pallas_call(
        write_out,
        out_shape=tuple(jax.ShapeDtypeStruct(shape, f32) for shape in shapes),
        in_specs=[pl.BlockSpec(memory_space=pltpu.VMEM)] * 3,
        out_specs=(hbm,) * 3,
        scratch_shapes=[dma((3, own))],
        compiler_params=pltpu.CompilerParams(vmem_limit_bytes=8 * 1024 * 1024),
    )(*[pltpu.with_memory_space_constraint(x, pltpu.VMEM) for x in results])


def solution(mesh):
    part = P("chain", "sector", None, None)
    term = P("chain", None, "sector", None, None)
    return jax.shard_map(
        on_device,
        mesh=mesh,
        in_specs=(part, P("chain", "sector"), P("chain", None), term, term, term, term, P()),
        out_specs=(part, term, term),
        check_vma=False,
    )
```

```python
import functools

import jax
import jax.numpy as jnp
from jax import lax
from jax.experimental import pallas as pl
from jax.experimental.pallas import tpu as pltpu
from jax.sharding import PartitionSpec as P

MESH = pl.DeviceIdType.MESH
STEPS = 3
OWN = 4
HOPS = 2
LATE = 4
SIZES = (8, 7, 6)
CHUNKS = 8
RELAY_LAG = CHUNKS - 2
LATE_LAG = 2
ENTRIES = tuple((i, j) for j in range(STEPS + 1) for i in range(j + 1))


def entry(i, j):
    return ENTRIES.index((min(i, j), max(i, j)))


def pair_dot(a, b):
    rows, cols = a.shape
    return jnp.sum((a * b).reshape(rows // 8, 8, cols), axis=0)


def quadratic(coef, other, gram, row_shift, col_shift):
    total = None
    for i, a in enumerate(coef):
        for j, b in enumerate(other):
            term = a * b * gram[entry(i + row_shift, j + col_shift)]
            total = term if total is None else total + term
    return total


def plan_kernel(source, plan, choice):
    need = []
    for d in range(4):
        mask = jnp.int32(0)
        for n in range(HOPS * OWN):
            mask = mask | (jnp.int32(1) << source[n // OWN, d * OWN + n % OWN])
        need.append(mask)
        plan[d] = mask

    def count(mask):
        mask = mask - ((mask >> 1) & 0x5555)
        mask = (mask & 0x3333) + ((mask >> 2) & 0x3333)
        mask = (mask + (mask >> 4)) & 0x0F0F
        return (mask + (mask >> 8)) & 0x1F

    most = count((need[2] | need[3]) & 0x00FF)
    for mask in ((need[0] | need[1]) & 0xFF00, need[3] & 0x0FFF, need[0] & 0xFFF0):
        most = jnp.maximum(most, count(mask))
    index = jnp.int32(0)
    for i, size in enumerate(SIZES):
        index = jnp.where(most <= size, jnp.int32(i), index)
    choice[0] = index


def kernel(
    size, rank, step_size, source, plan,
    psi_hbm, left_hbm, right_hbm, hop_left_hbm, hop_right_hbm,
    final, merged_left, merged_right,
    *scratch,
):
    f32, bf16 = jnp.float32, jnp.bfloat16
    per = STEPS * CHUNKS
    near_bufs, late_bufs, outer_bufs = (
        [scratch[(i * STEPS + k) * CHUNKS : (i * STEPS + k + 1) * CHUNKS] for k in range(STEPS)] for i in range(3)
    )
    at = 3 * per
    mid_early, mid_late, out_early, out_late = (scratch[at + i * STEPS : at + (i + 1) * STEPS] for i in range(4))
    at += 4 * STEPS
    first_part = size - LATE
    direct = first_part == OWN
    vec = scratch[at : at + STEPS + 1]
    at += STEPS + 1
    (psi, left, right, hop_left, hop_right, send_left, send_right, from_left, from_right, gram_acc, gram_in, gram_out, picks,
     load_sem, send_sem, recv_sem, gram_send, gram_recv, merge_send, merge_recv) = scratch[at:]

    me_c = lax.axis_index("chain")
    n_c = lax.axis_size("chain")
    z = lax.axis_index("sector")
    near = z + 1 - 2 * lax.rem(z, 2)
    peer = 3 - z
    far = 3 - near
    is_inner = jnp.logical_or(z == 1, z == 2)
    is_outer = jnp.logical_not(is_inner)
    nxt = lax.rem(me_c + 1, n_c)
    prv = lax.rem(me_c + n_c - 1, n_c)
    blk = psi.shape[1]
    rows = blk // CHUNKS
    chi = float(16 * blk)

    loads = [
        pltpu.make_async_copy(psi_hbm.at[0], psi, load_sem.at[0]),
        pltpu.make_async_copy(left_hbm.at[0], left, load_sem.at[1]),
        pltpu.make_async_copy(right_hbm.at[0], right, load_sem.at[2]),
        pltpu.make_async_copy(hop_left_hbm.at[0], hop_left, load_sem.at[3]),
        pltpu.make_async_copy(hop_right_hbm.at[0], hop_right, load_sem.at[4]),
    ]
    loads[0].start()

    barrier = pltpu.get_barrier_semaphore()
    for d in range(1, 4):
        pl.semaphore_signal(barrier, inc=1, device_id=(me_c, lax.rem(z + d, 4)), device_id_type=MESH)
    has_next = me_c < n_c - 1
    has_prev = me_c > 0

    @pl.when(has_prev)
    def _():
        pl.semaphore_signal(barrier, inc=1, device_id=(prv, z), device_id_type=MESH)

    @pl.when(has_next)
    def _():
        pl.semaphore_signal(barrier, inc=1, device_id=(nxt, z), device_id_type=MESH)


    row_at = lax.broadcasted_iota(jnp.int32, (blk, blk), 0)
    col_at = lax.broadcasted_iota(jnp.int32, (blk, blk), 1)

    def kept(j, value):
        r = rank[0, j]
        return jnp.where((row_at < r) & (col_at < r), value, 0.0)

    def put_own(k, j, value):
        value = value.astype(bf16)
        for c in range(CHUNKS):
            part = value[c * rows : (c + 1) * rows]
            near_bufs[k][c][4 + j] = part
            if not direct:
                for e in range(first_part):
                    mid_early[k][c, e] = part if j == 0 else jnp.where(picks[16 + e] == j, part, mid_early[k][c, e])

    def own_block(k, j):
        return jnp.concatenate([near_bufs[k][c][4 + j] for c in range(CHUNKS)], axis=0)

    def chunk_of(k, c, i):
        got = jnp.where(
            i < 8, near_bufs[k][c][jnp.minimum(i, 7)], late_bufs[k][c][jnp.minimum(jnp.maximum(i - 8, 0), 3)]
        )
        return jnp.where(i < 12, got, outer_bufs[k][c][jnp.maximum(i - 12, 0)])

    def near_or(k, c, i, other, start):
        return jnp.where(i < 8, near_bufs[k][c][jnp.minimum(i, 7)], other[k][c][jnp.maximum(i - start, 0)])

    def remote(src, dst, k, c, sent, received, to):
        return pltpu.make_async_remote_copy(
            src_ref=src, dst_ref=dst, send_sem=send_sem.at[k, c, sent], recv_sem=recv_sem.at[k, c, received],
            device_id=(me_c, to), device_id_type=MESH,
        )

    def arrive(k, c, late):
        return late_bufs[k][c] if late else near_bufs[k][c].at[0:first_part]

    def to_peer(k, c):
        src = near_bufs[k][c].at[4:8] if direct else mid_early[k].at[c]
        return remote(src, arrive(k, c, False), k, c, 0, 0, peer)

    def to_near(k, c):
        return remote(near_bufs[k][c].at[4:8], outer_bufs[k][c], k, c, 0, 2, near)

    def relay(k, c):
        return remote(mid_late[k].at[c], arrive(k, c, True), k, c, 1, 1, peer)

    def early(k, c):
        return remote(out_early[k].at[c], arrive(k, c, False), k, c, 2, 0, near)

    def late(k, c):
        return remote(out_late[k].at[c], arrive(k, c, True), k, c, 3, 1, near)

    def send_own(k):
        @pl.when(is_outer)
        def _():
            for c in range(CHUNKS):
                to_near(k, c).start()

        @pl.when(is_inner)
        def _():
            for c in range(CHUNKS):
                to_peer(k, c).start()

    zero, one = jnp.int32(0), jnp.int32(1)
    x = jnp.where(is_inner, z, near)
    y = 3 - x
    o = x + 1 - 2 * lax.rem(x, 2)
    yo = 3 - o

    def bits(mask, device):
        return [(mask >> (OWN * device + l)) & 1 for l in range(OWN)]

    def to_middle(a, ao, b, bo):
        mask = plan[b] | plan[bo]
        theirs, seen = [], zero
        for l, bit in enumerate(bits(mask, ao)):
            theirs.append((bit, 8 + seen, jnp.int32(12 + l)))
            seen = seen + bit
        mine, rank_l = [], zero
        for l, bit in enumerate(bits(mask, a)):
            if direct:
                mine.append((bit, jnp.int32(l), jnp.int32(4 + l)))
            else:
                row = jnp.where(rank_l < first_part, rank_l, 8 + seen + rank_l - first_part)
                mine.append((bit, row, jnp.int32(4 + l)))
                rank_l = rank_l + bit
        return mine, theirs

    sent_own, sent_outer = to_middle(x, o, y, yo)
    got_own, got_outer = to_middle(y, yo, x, o)

    def choose(items, row):
        pick = zero
        for bit, at_b, code in items:
            pick = jnp.where(jnp.logical_and(bit == 1, at_b == row), code, pick)
        return pick

    mask = plan[o]
    ready, seen, late_seen = [], zero, zero
    held = []
    for l, bit in enumerate(bits(mask, yo)):
        held.append((bit, 8 + late_seen, got_outer[l][1]))
        late_seen = late_seen + bit
    middle_late = []
    for l, bit in enumerate(bits(mask, y)):
        is_late = jnp.where(got_own[l][1] >= 8, bit, zero)
        middle_late.append((is_late, 8 + late_seen, got_own[l][1]))
        late_seen = late_seen + is_late
    for l, bit in enumerate(bits(mask, x)):
        ready.append((bit, seen, jnp.int32(4 + l)))
        seen = seen + bit
    for l, bit in enumerate(bits(mask, y)):
        is_early = jnp.where(got_own[l][1] < 8, bit, zero)
        ready.append((is_early, seen, got_own[l][1]))
        seen = seen + is_early
    ready = [
        (bit, jnp.where(at < first_part, at, 8 + late_seen + at - first_part), code) for bit, at, code in ready
    ]
    for l in range(OWN):
        picks[OWN * z + l] = jnp.int32(4 + l)
        picks[OWN * near + l] = jnp.where(is_inner, jnp.int32(12 + l), ready[l][1])
        at_o = jnp.where(middle_late[l][0] == 1, middle_late[l][1], ready[OWN + l][1])
        picks[OWN * y + l] = jnp.where(is_inner, got_own[l][1], at_o)
        picks[OWN * yo + l] = jnp.where(is_inner, got_outer[l][1], held[l][1])
    for e in range(OWN):
        picks[16 + e] = choose(sent_own, e) - 4
        picks[20 + e] = choose([*sent_own, *sent_outer], 8 + e)
        picks[24 + e] = choose(ready, e)
        picks[28 + e] = choose([*held, *middle_late, *ready], 8 + e)

    def exchange(k, meanwhile):
        for i in range(CHUNKS + RELAY_LAG + LATE_LAG):

            @pl.when(is_inner)
            def _():
                if i < CHUNKS:
                    to_peer(k, i).wait_recv()
                    for e in range(first_part):
                        out_early[k][i, e] = near_bufs[k][i][picks[24 + e]]
                    early(k, i).start()
                c = i - RELAY_LAG
                if 0 <= c < CHUNKS:
                    to_near(k, c).wait_recv()
                    for e in range(LATE):
                        mid_late[k][c, e] = near_or(k, c, picks[20 + e], outer_bufs, 12)
                    relay(k, c).start()
                c -= LATE_LAG
                if c >= 0:
                    relay(k, c).wait_recv()
                    for e in range(LATE):
                        out_late[k][c, e] = near_or(k, c, picks[28 + e], late_bufs, 8)
                    late(k, c).start()

            if i < OWN:
                meanwhile(i)

        @pl.when(is_outer)
        def _():
            for c in range(CHUNKS):
                early(k, c).wait_recv()
                late(k, c).wait_recv()

    def picked(k, b, j):
        i = picks[source[b, z * OWN + j]]
        return jnp.concatenate([chunk_of(k, c, i) for c in range(CHUNKS)], axis=0)

    def dot(a, b):
        return jnp.dot(a, b, preferred_element_type=f32)

    gram_acc[...] = jnp.zeros_like(gram_acc)
    loads[0].wait()
    for copy in loads[1:]:
        copy.start()

    for j in range(OWN):
        value = kept(j, psi[j])
        vec[0][j] = value
        put_own(0, j, value)
        gram_acc[entry(0, 0)] += pair_dot(value, value)

    pl.semaphore_wait(barrier, jnp.where(jnp.logical_and(has_prev, has_next), 5, 4))
    send_own(0)
    for copy in loads[1:3]:
        copy.wait()

    for k in range(STEPS):

        def on_site(j):
            half = dot(left[:, j].reshape(2 * blk, blk), own_block(k, j)).astype(bf16)
            both = jnp.concatenate([half[:blk], half[blk:]], axis=1)
            vec[k + 1][j] = dot(both, right[:, j].reshape(2 * blk, blk))

        exchange(k, on_site)
        if k == 0:
            for copy in loads[3:]:
                copy.wait()

        for j in range(OWN):
            both = jnp.concatenate(
                [dot(hop_left[b, j], picked(k, b, j)).astype(bf16) for b in range(HOPS)], axis=1
            )
            total = vec[k + 1][j] + dot(both, hop_right[:, j].reshape(2 * blk, blk))
            total = kept(j, total)
            vec[k + 1][j] = total
            if k + 1 < STEPS:
                put_own(k + 1, j, total)
            for i in range(k + 2):
                other = total if i == k + 1 else vec[i][j]
                gram_acc[entry(i, k + 1)] += pair_dot(total, other)
        if k + 1 < STEPS:
            send_own(k + 1)

    for e in range(len(ENTRIES)):
        line = jnp.sum(gram_acc[e], axis=0, keepdims=True)
        gram_out[e : e + 1, :] = line[:, :128] + line[:, 128:]
    gram_out[len(ENTRIES) :, :] = jnp.zeros((16 - len(ENTRIES), 128), f32)

    def gram_copy(d):
        return pltpu.make_async_remote_copy(
            src_ref=gram_out, dst_ref=gram_in.at[d - 1], send_sem=gram_send.at[d - 1],
            recv_sem=gram_recv.at[d - 1], device_id=(me_c, lax.rem(z + d, 4)), device_id_type=MESH,
        )

    for d in range(1, 4):
        gram_copy(d).start()
    for d in range(1, 4):
        gram_copy(d).wait_recv()
    gram_all = jnp.sum(gram_out[...] + gram_in[0] + gram_in[1] + gram_in[2], axis=1, keepdims=True)
    gram = [gram_all[e : e + 1] for e in range(len(ENTRIES))]

    coef = [jnp.ones((1, 1), f32)]
    for k in range(STEPS):
        h = step_size[0, k]
        self_dot = quadratic(coef, coef, gram, 0, 0)
        cross = quadratic(coef, coef, gram, 0, 1)
        grow = 1.0 + h * (cross / self_dot)
        new = [grow * c for c in coef] + [jnp.zeros((1, 1), f32)]
        for i, c in enumerate(coef):
            new[i + 1] = new[i + 1] - h * c
        scale = 1.0 / jnp.sqrt(quadratic(new, new, gram, 0, 0))
        coef = [c * scale for c in new]

    def merge(direction, a, j):
        src, dst, to = ((send_left, from_left, nxt), (send_right, from_right, prv))[direction]
        return pltpu.make_async_remote_copy(
            src_ref=src.at[a, j], dst_ref=dst.at[a, j], send_sem=merge_send.at[direction, a, j],
            recv_sem=merge_recv.at[direction, a, j], device_id=(to, z), device_id_type=MESH,
        )

    def finish(j, carry):
        value = coef[0] * vec[0][j]
        for i in range(1, STEPS + 1):
            value = value + coef[i] * vec[i][j]
        final[0, j] = value
        own = value.astype(bf16)
        own_t = value.T.astype(bf16)
        for a in range(2):
            half = dot(own_t, left[a, j]).astype(bf16)
            send_left[a, j] = (chi * dot(half, own)).astype(bf16)
            half = dot(right[a, j], own_t).astype(bf16)
            send_right[a, j] = (chi * dot(own, half)).astype(bf16)

        @pl.when(has_next)
        def _():
            for a in range(2):
                merge(0, a, j).start()

        @pl.when(has_prev)
        def _():
            for a in range(2):
                merge(1, a, j).start()

        return carry

    lax.fori_loop(0, OWN, finish, 0, unroll=True)
    def receive(direction, a, j, out, env, got):
        merge(direction, a, j).wait_recv()
        out[0, a, j] = env[a, j].astype(f32) + got[a, j].astype(f32)

    @pl.when(has_prev)
    def _():
        for j in range(OWN):
            for a in range(2):
                receive(0, a, j, merged_left, left, from_left)

    @pl.when(has_next)
    def _():
        for j in range(OWN):
            for a in range(2):
                receive(1, a, j, merged_right, right, from_right)

    @pl.when(jnp.logical_not(has_prev))
    def _():
        merged_left[0] = left[...].astype(f32)

    @pl.when(jnp.logical_not(has_next))
    def _():
        merged_right[0] = right[...].astype(f32)

    for k in range(STEPS):

        @pl.when(is_outer)
        def _():
            for c in range(CHUNKS):
                to_near(k, c).wait_send()

        @pl.when(is_inner)
        def _():
            for c in range(CHUNKS):
                to_peer(k, c).wait_send()
                relay(k, c).wait_send()
                early(k, c).wait_send()
                late(k, c).wait_send()

    for d in range(1, 4):
        gram_copy(d).wait_send()

    @pl.when(has_next)
    def _():
        for a in range(2):
            for j in range(OWN):
                merge(0, a, j).wait_send()

    @pl.when(has_prev)
    def _():
        for a in range(2):
            for j in range(OWN):
                merge(1, a, j).wait_send()


def write_out(*refs):
    count = (len(refs) - 1) // 2
    copies = [
        pltpu.make_async_copy(refs[i].at[0, j], refs[count + i].at[0, j], refs[-1].at[i, j])
        for i in range(count)
        for j in range(refs[i].shape[1])
    ]
    for copy in copies:
        copy.start()
    for copy in copies:
        copy.wait()


def window(index, plan, psi, kept_rank, step_size, left_env, right_env, hop_left, hop_right, hop_source):
    size = SIZES[index]
    f32, bf16 = jnp.float32, jnp.bfloat16
    own, blk = psi.shape[1], psi.shape[2]
    rows = blk // CHUNKS
    env = (2, own, blk, blk)
    smem = pl.BlockSpec(memory_space=pltpu.SMEM)
    hbm = pl.BlockSpec(memory_space=pl.ANY)
    dma = pltpu.SemaphoreType.DMA
    shapes = (psi.shape, left_env.shape, right_env.shape)
    held = [pltpu.with_memory_space_constraint(x, pltpu.HBM) for x in (psi, left_env, right_env, hop_left, hop_right)]
    results = pl.pallas_call(
        functools.partial(kernel, size),
        out_shape=tuple(pltpu.VMEM(shape, f32) for shape in shapes),
        in_specs=[smem] * 4 + [hbm] * 5,
        out_specs=(pl.BlockSpec(memory_space=pltpu.VMEM),) * 3,
        scratch_shapes=[
            *[pltpu.VMEM((8, rows, blk), bf16) for _ in range(STEPS * CHUNKS)],
            *[pltpu.VMEM((OWN, rows, blk), bf16) for _ in range(2 * STEPS * CHUNKS)],
            *[
                pltpu.VMEM((CHUNKS, count, rows, blk), bf16)
                for count in (size - LATE, LATE, size - LATE, LATE)
                for _ in range(STEPS)
            ],
            *[pltpu.VMEM((own, blk, blk), f32) for _ in range(STEPS + 1)],
            pltpu.VMEM((own, blk, blk), f32),
            *[pltpu.VMEM(env, bf16) for _ in range(4)],
            *[pltpu.VMEM(env, bf16) for _ in range(4)],
            pltpu.VMEM((len(ENTRIES), 8, blk), f32),
            pltpu.VMEM((3, 16, 128), f32),
            pltpu.VMEM((16, 128), f32),
            pltpu.SMEM((32,), jnp.int32),
            dma((5,)),
            dma((STEPS, CHUNKS, 4)),
            dma((STEPS, CHUNKS, 3)),
            dma((3,)),
            dma((3,)),
            dma((2, 2, own)),
            dma((2, 2, own)),
        ],
        compiler_params=pltpu.CompilerParams(
            collective_id=index, has_side_effects=True, vmem_limit_bytes=61_700_000
        ),
    )(kept_rank, step_size, hop_source, plan, *held)
    return pl.pallas_call(
        write_out,
        out_shape=tuple(jax.ShapeDtypeStruct(shape, f32) for shape in shapes),
        in_specs=[pl.BlockSpec(memory_space=pltpu.VMEM)] * 3,
        out_specs=(hbm,) * 3,
        scratch_shapes=[dma((3, own))],
        compiler_params=pltpu.CompilerParams(vmem_limit_bytes=8 * 1024 * 1024),
    )(*[pltpu.with_memory_space_constraint(x, pltpu.VMEM) for x in results])


def on_device(*args):
    smem = pl.BlockSpec(memory_space=pltpu.SMEM)
    plan, choice = pl.pallas_call(
        plan_kernel,
        out_shape=(jax.ShapeDtypeStruct((4,), jnp.int32), jax.ShapeDtypeStruct((1,), jnp.int32)),
        in_specs=[smem],
        out_specs=(smem, smem),
    )(args[-1])
    return lax.switch(choice.reshape(()), [functools.partial(window, i) for i in range(len(SIZES))], plan, *args)


def solution(mesh):
    part = P("chain", "sector", None, None)
    term = P("chain", None, "sector", None, None)
    return jax.shard_map(
        on_device,
        mesh=mesh,
        in_specs=(part, P("chain", "sector"), P("chain", None), term, term, term, term, P()),
        out_specs=(part, term, term),
        check_vma=False,
    )
```

```python
import functools

import jax
import jax.numpy as jnp
from jax import lax
from jax.experimental import pallas as pl
from jax.experimental.pallas import tpu as pltpu
from jax.sharding import PartitionSpec as P

MESH = pl.DeviceIdType.MESH
STEPS = 3
OWN = 4
HOPS = 2
LATE = 4
SIZES = (8, 7, 6)
CHUNKS = 8
RELAY_LAG = CHUNKS - 2
LATE_LAG = 3
ENTRIES = tuple((i, j) for j in range(STEPS + 1) for i in range(j + 1))


def entry(i, j):
    return ENTRIES.index((min(i, j), max(i, j)))


def pair_dot(a, b):
    rows, cols = a.shape
    return jnp.sum((a * b).reshape(rows // 8, 8, cols), axis=0)


def quadratic(coef, other, gram, row_shift, col_shift):
    total = None
    for i, a in enumerate(coef):
        for j, b in enumerate(other):
            term = a * b * gram[entry(i + row_shift, j + col_shift)]
            total = term if total is None else total + term
    return total


def plan_kernel(source, plan, choice):
    need = []
    for d in range(4):
        mask = jnp.int32(0)
        for n in range(HOPS * OWN):
            mask = mask | (jnp.int32(1) << source[n // OWN, d * OWN + n % OWN])
        need.append(mask)
        plan[d] = mask

    def count(mask):
        mask = mask - ((mask >> 1) & 0x5555)
        mask = (mask & 0x3333) + ((mask >> 2) & 0x3333)
        mask = (mask + (mask >> 4)) & 0x0F0F
        return (mask + (mask >> 8)) & 0x1F

    most = count((need[2] | need[3]) & 0x00FF)
    for mask in ((need[0] | need[1]) & 0xFF00, need[3] & 0x0FFF, need[0] & 0xFFF0):
        most = jnp.maximum(most, count(mask))
    index = jnp.int32(0)
    for i, size in enumerate(SIZES):
        index = jnp.where(most <= size, jnp.int32(i), index)
    choice[0] = index


def kernel(
    size, rank, step_size, source, plan,
    psi_hbm, left_hbm, right_hbm, hop_left_hbm, hop_right_hbm,
    final, merged_left, merged_right,
    *scratch,
):
    f32, bf16 = jnp.float32, jnp.bfloat16
    per = STEPS * CHUNKS
    near_bufs, late_bufs, outer_bufs = (
        [scratch[(i * STEPS + k) * CHUNKS : (i * STEPS + k + 1) * CHUNKS] for k in range(STEPS)] for i in range(3)
    )
    at = 3 * per
    mid_early, mid_late, out_early, out_late = (scratch[at + i * STEPS : at + (i + 1) * STEPS] for i in range(4))
    at += 4 * STEPS
    first_part = size - LATE
    direct = first_part == OWN
    vec = scratch[at : at + STEPS + 1]
    at += STEPS + 1
    (psi, left, right, hop_left, hop_right, send_left, send_right, from_left, from_right, gram_acc, gram_in, gram_out, picks,
     load_sem, send_sem, recv_sem, gram_send, gram_recv, merge_send, merge_recv) = scratch[at:]

    me_c = lax.axis_index("chain")
    n_c = lax.axis_size("chain")
    z = lax.axis_index("sector")
    near = z + 1 - 2 * lax.rem(z, 2)
    peer = 3 - z
    far = 3 - near
    is_inner = jnp.logical_or(z == 1, z == 2)
    is_outer = jnp.logical_not(is_inner)
    nxt = lax.rem(me_c + 1, n_c)
    prv = lax.rem(me_c + n_c - 1, n_c)
    blk = psi.shape[1]
    rows = blk // CHUNKS
    chi = float(16 * blk)

    loads = [
        pltpu.make_async_copy(psi_hbm.at[0], psi, load_sem.at[0]),
        pltpu.make_async_copy(left_hbm.at[0], left, load_sem.at[1]),
        pltpu.make_async_copy(right_hbm.at[0], right, load_sem.at[2]),
        pltpu.make_async_copy(hop_left_hbm.at[0], hop_left, load_sem.at[3]),
        pltpu.make_async_copy(hop_right_hbm.at[0], hop_right, load_sem.at[4]),
    ]
    loads[0].start()

    barrier = pltpu.get_barrier_semaphore()
    for d in range(1, 4):
        pl.semaphore_signal(barrier, inc=1, device_id=(me_c, lax.rem(z + d, 4)), device_id_type=MESH)
    has_next = me_c < n_c - 1
    has_prev = me_c > 0

    @pl.when(has_prev)
    def _():
        pl.semaphore_signal(barrier, inc=1, device_id=(prv, z), device_id_type=MESH)

    @pl.when(has_next)
    def _():
        pl.semaphore_signal(barrier, inc=1, device_id=(nxt, z), device_id_type=MESH)


    row_at = lax.broadcasted_iota(jnp.int32, (blk, blk), 0)
    col_at = lax.broadcasted_iota(jnp.int32, (blk, blk), 1)

    def kept(j, value):
        r = rank[0, j]
        return jnp.where((row_at < r) & (col_at < r), value, 0.0)

    def put_own(k, j, value):
        value = value.astype(bf16)
        for c in range(CHUNKS):
            part = value[c * rows : (c + 1) * rows]
            near_bufs[k][c][4 + j] = part
            if not direct:
                for e in range(first_part):
                    mid_early[k][c, e] = part if j == 0 else jnp.where(picks[16 + e] == j, part, mid_early[k][c, e])

    def own_block(k, j):
        return jnp.concatenate([near_bufs[k][c][4 + j] for c in range(CHUNKS)], axis=0)

    def chunk_of(k, c, i):
        got = jnp.where(
            i < 8, near_bufs[k][c][jnp.minimum(i, 7)], late_bufs[k][c][jnp.minimum(jnp.maximum(i - 8, 0), 3)]
        )
        return jnp.where(i < 12, got, outer_bufs[k][c][jnp.maximum(i - 12, 0)])

    def near_or(k, c, i, other, start):
        return jnp.where(i < 8, near_bufs[k][c][jnp.minimum(i, 7)], other[k][c][jnp.maximum(i - start, 0)])

    def remote(src, dst, k, c, sent, received, to):
        return pltpu.make_async_remote_copy(
            src_ref=src, dst_ref=dst, send_sem=send_sem.at[k, c, sent], recv_sem=recv_sem.at[k, c, received],
            device_id=(me_c, to), device_id_type=MESH,
        )

    def arrive(k, c, late):
        return late_bufs[k][c] if late else near_bufs[k][c].at[0:first_part]

    def to_peer(k, c):
        src = near_bufs[k][c].at[4:8] if direct else mid_early[k].at[c]
        return remote(src, arrive(k, c, False), k, c, 0, 0, peer)

    def to_near(k, c):
        return remote(near_bufs[k][c].at[4:8], outer_bufs[k][c], k, c, 0, 2, near)

    def relay(k, c):
        return remote(mid_late[k].at[c], arrive(k, c, True), k, c, 1, 1, peer)

    def early(k, c):
        return remote(out_early[k].at[c], arrive(k, c, False), k, c, 2, 0, near)

    def late(k, c):
        return remote(out_late[k].at[c], arrive(k, c, True), k, c, 3, 1, near)

    def send_own(k):
        @pl.when(is_outer)
        def _():
            for c in range(CHUNKS):
                to_near(k, c).start()

        @pl.when(is_inner)
        def _():
            for c in range(CHUNKS):
                to_peer(k, c).start()

    zero, one = jnp.int32(0), jnp.int32(1)
    x = jnp.where(is_inner, z, near)
    y = 3 - x
    o = x + 1 - 2 * lax.rem(x, 2)
    yo = 3 - o

    def bits(mask, device):
        return [(mask >> (OWN * device + l)) & 1 for l in range(OWN)]

    def to_middle(a, ao, b, bo):
        mask = plan[b] | plan[bo]
        theirs, seen = [], zero
        for l, bit in enumerate(bits(mask, ao)):
            theirs.append((bit, 8 + seen, jnp.int32(12 + l)))
            seen = seen + bit
        mine, rank_l = [], zero
        for l, bit in enumerate(bits(mask, a)):
            if direct:
                mine.append((bit, jnp.int32(l), jnp.int32(4 + l)))
            else:
                row = jnp.where(rank_l < first_part, rank_l, 8 + seen + rank_l - first_part)
                mine.append((bit, row, jnp.int32(4 + l)))
                rank_l = rank_l + bit
        return mine, theirs

    sent_own, sent_outer = to_middle(x, o, y, yo)
    got_own, got_outer = to_middle(y, yo, x, o)

    def choose(items, row):
        pick = zero
        for bit, at_b, code in items:
            pick = jnp.where(jnp.logical_and(bit == 1, at_b == row), code, pick)
        return pick

    mask = plan[o]
    ready, seen, late_seen = [], zero, zero
    held = []
    for l, bit in enumerate(bits(mask, yo)):
        held.append((bit, 8 + late_seen, got_outer[l][1]))
        late_seen = late_seen + bit
    middle_late = []
    for l, bit in enumerate(bits(mask, y)):
        is_late = jnp.where(got_own[l][1] >= 8, bit, zero)
        middle_late.append((is_late, 8 + late_seen, got_own[l][1]))
        late_seen = late_seen + is_late
    for l, bit in enumerate(bits(mask, x)):
        ready.append((bit, seen, jnp.int32(4 + l)))
        seen = seen + bit
    for l, bit in enumerate(bits(mask, y)):
        is_early = jnp.where(got_own[l][1] < 8, bit, zero)
        ready.append((is_early, seen, got_own[l][1]))
        seen = seen + is_early
    ready = [
        (bit, jnp.where(at < first_part, at, 8 + late_seen + at - first_part), code) for bit, at, code in ready
    ]
    for l in range(OWN):
        picks[OWN * z + l] = jnp.int32(4 + l)
        picks[OWN * near + l] = jnp.where(is_inner, jnp.int32(12 + l), ready[l][1])
        at_o = jnp.where(middle_late[l][0] == 1, middle_late[l][1], ready[OWN + l][1])
        picks[OWN * y + l] = jnp.where(is_inner, got_own[l][1], at_o)
        picks[OWN * yo + l] = jnp.where(is_inner, got_outer[l][1], held[l][1])
    for e in range(OWN):
        picks[16 + e] = choose(sent_own, e) - 4
        picks[20 + e] = choose([*sent_own, *sent_outer], 8 + e)
        picks[24 + e] = choose(ready, e)
        picks[28 + e] = choose([*held, *middle_late, *ready], 8 + e)

    def exchange(k, meanwhile):
        for i in range(CHUNKS + RELAY_LAG + LATE_LAG):

            @pl.when(is_inner)
            def _():
                if i < CHUNKS:
                    to_peer(k, i).wait_recv()
                    for e in range(first_part):
                        out_early[k][i, e] = near_bufs[k][i][picks[24 + e]]
                    early(k, i).start()
                c = i - RELAY_LAG
                if 0 <= c < CHUNKS:
                    to_near(k, c).wait_recv()
                    for e in range(LATE):
                        mid_late[k][c, e] = near_or(k, c, picks[20 + e], outer_bufs, 12)
                    relay(k, c).start()
                c -= LATE_LAG
                if c >= 0:
                    relay(k, c).wait_recv()
                    for e in range(LATE):
                        out_late[k][c, e] = near_or(k, c, picks[28 + e], late_bufs, 8)
                    late(k, c).start()

            if i < OWN:
                meanwhile(i)

        @pl.when(is_outer)
        def _():
            for c in range(CHUNKS):
                early(k, c).wait_recv()
                late(k, c).wait_recv()

    def picked(k, b, j):
        i = picks[source[b, z * OWN + j]]
        return jnp.concatenate([chunk_of(k, c, i) for c in range(CHUNKS)], axis=0)

    def dot(a, b):
        return jnp.dot(a, b, preferred_element_type=f32)

    gram_acc[...] = jnp.zeros_like(gram_acc)
    loads[0].wait()
    for copy in loads[1:]:
        copy.start()

    for j in range(OWN):
        value = kept(j, psi[j])
        vec[0][j] = value
        put_own(0, j, value)
        gram_acc[entry(0, 0)] += pair_dot(value, value)

    pl.semaphore_wait(barrier, jnp.where(jnp.logical_and(has_prev, has_next), 5, 4))
    send_own(0)
    for copy in loads[1:3]:
        copy.wait()

    for k in range(STEPS):

        def on_site(j):
            half = dot(left[:, j].reshape(2 * blk, blk), own_block(k, j)).astype(bf16)
            both = jnp.concatenate([half[:blk], half[blk:]], axis=1)
            vec[k + 1][j] = dot(both, right[:, j].reshape(2 * blk, blk))

        exchange(k, on_site)
        if k == 0:
            for copy in loads[3:]:
                copy.wait()

        for j in range(OWN):
            both = jnp.concatenate(
                [dot(hop_left[b, j], picked(k, b, j)).astype(bf16) for b in range(HOPS)], axis=1
            )
            total = vec[k + 1][j] + dot(both, hop_right[:, j].reshape(2 * blk, blk))
            total = kept(j, total)
            vec[k + 1][j] = total
            if k + 1 < STEPS:
                put_own(k + 1, j, total)
            for i in range(k + 2):
                other = total if i == k + 1 else vec[i][j]
                gram_acc[entry(i, k + 1)] += pair_dot(total, other)
        if k + 1 < STEPS:
            send_own(k + 1)

    for e in range(len(ENTRIES)):
        line = jnp.sum(gram_acc[e], axis=0, keepdims=True)
        gram_out[e : e + 1, :] = line[:, :128] + line[:, 128:]
    gram_out[len(ENTRIES) :, :] = jnp.zeros((16 - len(ENTRIES), 128), f32)

    def gram_copy(d):
        return pltpu.make_async_remote_copy(
            src_ref=gram_out, dst_ref=gram_in.at[d - 1], send_sem=gram_send.at[d - 1],
            recv_sem=gram_recv.at[d - 1], device_id=(me_c, lax.rem(z + d, 4)), device_id_type=MESH,
        )

    for d in range(1, 4):
        gram_copy(d).start()
    for d in range(1, 4):
        gram_copy(d).wait_recv()
    gram_all = jnp.sum(gram_out[...] + gram_in[0] + gram_in[1] + gram_in[2], axis=1, keepdims=True)
    gram = [gram_all[e : e + 1] for e in range(len(ENTRIES))]

    coef = [jnp.ones((1, 1), f32)]
    for k in range(STEPS):
        h = step_size[0, k]
        self_dot = quadratic(coef, coef, gram, 0, 0)
        cross = quadratic(coef, coef, gram, 0, 1)
        grow = 1.0 + h * (cross / self_dot)
        new = [grow * c for c in coef] + [jnp.zeros((1, 1), f32)]
        for i, c in enumerate(coef):
            new[i + 1] = new[i + 1] - h * c
        scale = 1.0 / jnp.sqrt(quadratic(new, new, gram, 0, 0))
        coef = [c * scale for c in new]

    def merge(direction, j):
        src, dst, to = ((send_left, from_left, nxt), (send_right, from_right, prv))[direction]
        return pltpu.make_async_remote_copy(
            src_ref=src.at[j], dst_ref=dst.at[j], send_sem=merge_send.at[direction, j],
            recv_sem=merge_recv.at[direction, j], device_id=(to, z), device_id_type=MESH,
        )

    def finish(j, carry):
        value = coef[0] * vec[0][j]
        for i in range(1, STEPS + 1):
            value = value + coef[i] * vec[i][j]
        final[0, j] = value
        own = value.astype(bf16)
        own_t = value.T.astype(bf16)
        for a in range(2):
            half = dot(own_t, left[a, j]).astype(bf16)
            send_left[j, a] = (chi * dot(half, own)).astype(bf16)
            half = dot(right[a, j], own_t).astype(bf16)
            send_right[j, a] = (chi * dot(own, half)).astype(bf16)

        @pl.when(has_next)
        def _():
            merge(0, j).start()

        @pl.when(has_prev)
        def _():
            merge(1, j).start()

        return carry

    lax.fori_loop(0, OWN, finish, 0, unroll=True)
    def receive(direction, j, out, env, got):
        merge(direction, j).wait_recv()
        for a in range(2):
            out[0, a, j] = env[a, j].astype(f32) + got[j, a].astype(f32)

    @pl.when(has_prev)
    def _():
        for j in range(OWN):
            receive(0, j, merged_left, left, from_left)

    @pl.when(has_next)
    def _():
        for j in range(OWN):
            receive(1, j, merged_right, right, from_right)

    @pl.when(jnp.logical_not(has_prev))
    def _():
        merged_left[0] = left[...].astype(f32)

    @pl.when(jnp.logical_not(has_next))
    def _():
        merged_right[0] = right[...].astype(f32)

    for k in range(STEPS):

        @pl.when(is_outer)
        def _():
            for c in range(CHUNKS):
                to_near(k, c).wait_send()

        @pl.when(is_inner)
        def _():
            for c in range(CHUNKS):
                to_peer(k, c).wait_send()
                relay(k, c).wait_send()
                early(k, c).wait_send()
                late(k, c).wait_send()

    for d in range(1, 4):
        gram_copy(d).wait_send()

    @pl.when(has_next)
    def _():
        for j in range(OWN):
            merge(0, j).wait_send()

    @pl.when(has_prev)
    def _():
        for j in range(OWN):
            merge(1, j).wait_send()


def write_out(*refs):
    count = (len(refs) - 1) // 2
    copies = [
        pltpu.make_async_copy(refs[i].at[0, j], refs[count + i].at[0, j], refs[-1].at[i, j])
        for i in range(count)
        for j in range(refs[i].shape[1])
    ]
    for copy in copies:
        copy.start()
    for copy in copies:
        copy.wait()


def window(index, plan, psi, kept_rank, step_size, left_env, right_env, hop_left, hop_right, hop_source):
    size = SIZES[index]
    f32, bf16 = jnp.float32, jnp.bfloat16
    own, blk = psi.shape[1], psi.shape[2]
    rows = blk // CHUNKS
    env = (2, own, blk, blk)
    smem = pl.BlockSpec(memory_space=pltpu.SMEM)
    hbm = pl.BlockSpec(memory_space=pl.ANY)
    dma = pltpu.SemaphoreType.DMA
    shapes = (psi.shape, left_env.shape, right_env.shape)
    held = [pltpu.with_memory_space_constraint(x, pltpu.HBM) for x in (psi, left_env, right_env, hop_left, hop_right)]
    results = pl.pallas_call(
        functools.partial(kernel, size),
        out_shape=tuple(pltpu.VMEM(shape, f32) for shape in shapes),
        in_specs=[smem] * 4 + [hbm] * 5,
        out_specs=(pl.BlockSpec(memory_space=pltpu.VMEM),) * 3,
        scratch_shapes=[
            *[pltpu.VMEM((8, rows, blk), bf16) for _ in range(STEPS * CHUNKS)],
            *[pltpu.VMEM((OWN, rows, blk), bf16) for _ in range(2 * STEPS * CHUNKS)],
            *[
                pltpu.VMEM((CHUNKS, count, rows, blk), bf16)
                for count in (size - LATE, LATE, size - LATE, LATE)
                for _ in range(STEPS)
            ],
            *[pltpu.VMEM((own, blk, blk), f32) for _ in range(STEPS + 1)],
            pltpu.VMEM((own, blk, blk), f32),
            *[pltpu.VMEM(env, bf16) for _ in range(4)],
            *[pltpu.VMEM((own, 2, blk, blk), bf16) for _ in range(4)],
            pltpu.VMEM((len(ENTRIES), 8, blk), f32),
            pltpu.VMEM((3, 16, 128), f32),
            pltpu.VMEM((16, 128), f32),
            pltpu.SMEM((32,), jnp.int32),
            dma((5,)),
            dma((STEPS, CHUNKS, 4)),
            dma((STEPS, CHUNKS, 3)),
            dma((3,)),
            dma((3,)),
            dma((2, own)),
            dma((2, own)),
        ],
        compiler_params=pltpu.CompilerParams(
            collective_id=index, has_side_effects=True, vmem_limit_bytes=61_700_000
        ),
    )(kept_rank, step_size, hop_source, plan, *held)
    return pl.pallas_call(
        write_out,
        out_shape=tuple(jax.ShapeDtypeStruct(shape, f32) for shape in shapes),
        in_specs=[pl.BlockSpec(memory_space=pltpu.VMEM)] * 3,
        out_specs=(hbm,) * 3,
        scratch_shapes=[dma((3, own))],
        compiler_params=pltpu.CompilerParams(vmem_limit_bytes=8 * 1024 * 1024),
    )(*[pltpu.with_memory_space_constraint(x, pltpu.VMEM) for x in results])


def on_device(*args):
    smem = pl.BlockSpec(memory_space=pltpu.SMEM)
    plan, choice = pl.pallas_call(
        plan_kernel,
        out_shape=(jax.ShapeDtypeStruct((4,), jnp.int32), jax.ShapeDtypeStruct((1,), jnp.int32)),
        in_specs=[smem],
        out_specs=(smem, smem),
    )(args[-1])
    return lax.switch(choice.reshape(()), [functools.partial(window, i) for i in range(len(SIZES))], plan, *args)


def solution(mesh):
    part = P("chain", "sector", None, None)
    term = P("chain", None, "sector", None, None)
    return jax.shard_map(
        on_device,
        mesh=mesh,
        in_specs=(part, P("chain", "sector"), P("chain", None), term, term, term, term, P()),
        out_specs=(part, term, term),
        check_vma=False,
    )
```

```python
import functools

import jax
import jax.numpy as jnp
from jax import lax
from jax.experimental import pallas as pl
from jax.experimental.pallas import tpu as pltpu
from jax.sharding import PartitionSpec as P

MESH = pl.DeviceIdType.MESH
STEPS = 3
OWN = 4
HOPS = 2
LATE = 4
SIZES = (8, 7, 6)
CHUNKS = 8
RELAY_LAG = CHUNKS - 3
LATE_LAG = 4
ENTRIES = tuple((i, j) for j in range(STEPS + 1) for i in range(j + 1))


def entry(i, j):
    return ENTRIES.index((min(i, j), max(i, j)))


def pair_dot(a, b):
    rows, cols = a.shape
    return jnp.sum((a * b).reshape(rows // 8, 8, cols), axis=0)


def quadratic(coef, other, gram, row_shift, col_shift):
    total = None
    for i, a in enumerate(coef):
        for j, b in enumerate(other):
            term = a * b * gram[entry(i + row_shift, j + col_shift)]
            total = term if total is None else total + term
    return total


def plan_kernel(source, plan, choice):
    need = []
    for d in range(4):
        mask = jnp.int32(0)
        for n in range(HOPS * OWN):
            mask = mask | (jnp.int32(1) << source[n // OWN, d * OWN + n % OWN])
        need.append(mask)
        plan[d] = mask

    def count(mask):
        mask = mask - ((mask >> 1) & 0x5555)
        mask = (mask & 0x3333) + ((mask >> 2) & 0x3333)
        mask = (mask + (mask >> 4)) & 0x0F0F
        return (mask + (mask >> 8)) & 0x1F

    most = count((need[2] | need[3]) & 0x00FF)
    for mask in ((need[0] | need[1]) & 0xFF00, need[3] & 0x0FFF, need[0] & 0xFFF0):
        most = jnp.maximum(most, count(mask))
    index = jnp.int32(0)
    for i, size in enumerate(SIZES):
        index = jnp.where(most <= size, jnp.int32(i), index)
    choice[0] = index


def kernel(
    size, rank, step_size, source, plan,
    psi_hbm, left_hbm, right_hbm, hop_left_hbm, hop_right_hbm,
    final, merged_left, merged_right,
    *scratch,
):
    f32, bf16 = jnp.float32, jnp.bfloat16
    per = STEPS * CHUNKS
    near_bufs, late_bufs, outer_bufs = (
        [scratch[(i * STEPS + k) * CHUNKS : (i * STEPS + k + 1) * CHUNKS] for k in range(STEPS)] for i in range(3)
    )
    at = 3 * per
    mid_early, mid_late, out_early, out_late = (scratch[at + i * STEPS : at + (i + 1) * STEPS] for i in range(4))
    at += 4 * STEPS
    first_part = size - LATE
    direct = first_part == OWN
    vec = scratch[at : at + STEPS + 1]
    at += STEPS + 1
    (psi, left, right, hop_left, hop_right, send_left, send_right, from_left, from_right, gram_acc, gram_in, gram_out, picks,
     load_sem, send_sem, recv_sem, gram_send, gram_recv, merge_send, merge_recv) = scratch[at:]

    me_c = lax.axis_index("chain")
    n_c = lax.axis_size("chain")
    z = lax.axis_index("sector")
    near = z + 1 - 2 * lax.rem(z, 2)
    peer = 3 - z
    far = 3 - near
    is_inner = jnp.logical_or(z == 1, z == 2)
    is_outer = jnp.logical_not(is_inner)
    nxt = lax.rem(me_c + 1, n_c)
    prv = lax.rem(me_c + n_c - 1, n_c)
    blk = psi.shape[1]
    rows = blk // CHUNKS
    chi = float(16 * blk)

    loads = [
        pltpu.make_async_copy(psi_hbm.at[0], psi, load_sem.at[0]),
        pltpu.make_async_copy(left_hbm.at[0], left, load_sem.at[1]),
        pltpu.make_async_copy(right_hbm.at[0], right, load_sem.at[2]),
        pltpu.make_async_copy(hop_left_hbm.at[0], hop_left, load_sem.at[3]),
        pltpu.make_async_copy(hop_right_hbm.at[0], hop_right, load_sem.at[4]),
    ]
    loads[0].start()

    barrier = pltpu.get_barrier_semaphore()
    for d in range(1, 4):
        pl.semaphore_signal(barrier, inc=1, device_id=(me_c, lax.rem(z + d, 4)), device_id_type=MESH)
    has_next = me_c < n_c - 1
    has_prev = me_c > 0

    @pl.when(has_prev)
    def _():
        pl.semaphore_signal(barrier, inc=1, device_id=(prv, z), device_id_type=MESH)

    @pl.when(has_next)
    def _():
        pl.semaphore_signal(barrier, inc=1, device_id=(nxt, z), device_id_type=MESH)


    row_at = lax.broadcasted_iota(jnp.int32, (blk, blk), 0)
    col_at = lax.broadcasted_iota(jnp.int32, (blk, blk), 1)

    def kept(j, value):
        r = rank[0, j]
        return jnp.where((row_at < r) & (col_at < r), value, 0.0)

    def put_own(k, j, value):
        value = value.astype(bf16)
        for c in range(CHUNKS):
            part = value[c * rows : (c + 1) * rows]
            near_bufs[k][c][4 + j] = part
            if not direct:
                for e in range(first_part):
                    mid_early[k][c, e] = part if j == 0 else jnp.where(picks[16 + e] == j, part, mid_early[k][c, e])

    def own_block(k, j):
        return jnp.concatenate([near_bufs[k][c][4 + j] for c in range(CHUNKS)], axis=0)

    def chunk_of(k, c, i):
        got = jnp.where(
            i < 8, near_bufs[k][c][jnp.minimum(i, 7)], late_bufs[k][c][jnp.minimum(jnp.maximum(i - 8, 0), 3)]
        )
        return jnp.where(i < 12, got, outer_bufs[k][c][jnp.maximum(i - 12, 0)])

    def near_or(k, c, i, other, start):
        return jnp.where(i < 8, near_bufs[k][c][jnp.minimum(i, 7)], other[k][c][jnp.maximum(i - start, 0)])

    def remote(src, dst, k, c, sent, received, to):
        return pltpu.make_async_remote_copy(
            src_ref=src, dst_ref=dst, send_sem=send_sem.at[k, c, sent], recv_sem=recv_sem.at[k, c, received],
            device_id=(me_c, to), device_id_type=MESH,
        )

    def arrive(k, c, late):
        return late_bufs[k][c] if late else near_bufs[k][c].at[0:first_part]

    def to_peer(k, c):
        src = near_bufs[k][c].at[4:8] if direct else mid_early[k].at[c]
        return remote(src, arrive(k, c, False), k, c, 0, 0, peer)

    def to_near(k, c):
        return remote(near_bufs[k][c].at[4:8], outer_bufs[k][c], k, c, 0, 2, near)

    def relay(k, c):
        return remote(mid_late[k].at[c], arrive(k, c, True), k, c, 1, 1, peer)

    def early(k, c):
        return remote(out_early[k].at[c], arrive(k, c, False), k, c, 2, 0, near)

    def late(k, c):
        return remote(out_late[k].at[c], arrive(k, c, True), k, c, 3, 1, near)

    def send_own(k):
        @pl.when(is_outer)
        def _():
            for c in range(CHUNKS):
                to_near(k, c).start()

        @pl.when(is_inner)
        def _():
            for c in range(CHUNKS):
                to_peer(k, c).start()

    zero, one = jnp.int32(0), jnp.int32(1)
    x = jnp.where(is_inner, z, near)
    y = 3 - x
    o = x + 1 - 2 * lax.rem(x, 2)
    yo = 3 - o

    def bits(mask, device):
        return [(mask >> (OWN * device + l)) & 1 for l in range(OWN)]

    def to_middle(a, ao, b, bo):
        mask = plan[b] | plan[bo]
        theirs, seen = [], zero
        for l, bit in enumerate(bits(mask, ao)):
            theirs.append((bit, 8 + seen, jnp.int32(12 + l)))
            seen = seen + bit
        mine, rank_l = [], zero
        for l, bit in enumerate(bits(mask, a)):
            if direct:
                mine.append((bit, jnp.int32(l), jnp.int32(4 + l)))
            else:
                row = jnp.where(rank_l < first_part, rank_l, 8 + seen + rank_l - first_part)
                mine.append((bit, row, jnp.int32(4 + l)))
                rank_l = rank_l + bit
        return mine, theirs

    sent_own, sent_outer = to_middle(x, o, y, yo)
    got_own, got_outer = to_middle(y, yo, x, o)

    def choose(items, row):
        pick = zero
        for bit, at_b, code in items:
            pick = jnp.where(jnp.logical_and(bit == 1, at_b == row), code, pick)
        return pick

    mask = plan[o]
    ready, seen, late_seen = [], zero, zero
    held = []
    for l, bit in enumerate(bits(mask, yo)):
        held.append((bit, 8 + late_seen, got_outer[l][1]))
        late_seen = late_seen + bit
    middle_late = []
    for l, bit in enumerate(bits(mask, y)):
        is_late = jnp.where(got_own[l][1] >= 8, bit, zero)
        middle_late.append((is_late, 8 + late_seen, got_own[l][1]))
        late_seen = late_seen + is_late
    for l, bit in enumerate(bits(mask, x)):
        ready.append((bit, seen, jnp.int32(4 + l)))
        seen = seen + bit
    for l, bit in enumerate(bits(mask, y)):
        is_early = jnp.where(got_own[l][1] < 8, bit, zero)
        ready.append((is_early, seen, got_own[l][1]))
        seen = seen + is_early
    ready = [
        (bit, jnp.where(at < first_part, at, 8 + late_seen + at - first_part), code) for bit, at, code in ready
    ]
    for l in range(OWN):
        picks[OWN * z + l] = jnp.int32(4 + l)
        picks[OWN * near + l] = jnp.where(is_inner, jnp.int32(12 + l), ready[l][1])
        at_o = jnp.where(middle_late[l][0] == 1, middle_late[l][1], ready[OWN + l][1])
        picks[OWN * y + l] = jnp.where(is_inner, got_own[l][1], at_o)
        picks[OWN * yo + l] = jnp.where(is_inner, got_outer[l][1], held[l][1])
    for e in range(OWN):
        picks[16 + e] = choose(sent_own, e) - 4
        picks[20 + e] = choose([*sent_own, *sent_outer], 8 + e)
        picks[24 + e] = choose(ready, e)
        picks[28 + e] = choose([*held, *middle_late, *ready], 8 + e)

    def exchange(k, meanwhile):
        for i in range(CHUNKS + RELAY_LAG + LATE_LAG):

            @pl.when(is_inner)
            def _():
                if i < CHUNKS:
                    to_peer(k, i).wait_recv()
                    for e in range(first_part):
                        out_early[k][i, e] = near_bufs[k][i][picks[24 + e]]
                    early(k, i).start()
                c = i - RELAY_LAG
                if 0 <= c < CHUNKS:
                    to_near(k, c).wait_recv()
                    for e in range(LATE):
                        mid_late[k][c, e] = near_or(k, c, picks[20 + e], outer_bufs, 12)
                    relay(k, c).start()
                c -= LATE_LAG
                if c >= 0:
                    relay(k, c).wait_recv()
                    for e in range(LATE):
                        out_late[k][c, e] = near_or(k, c, picks[28 + e], late_bufs, 8)
                    late(k, c).start()

            if i < OWN:
                meanwhile(i)

        @pl.when(is_outer)
        def _():
            for c in range(CHUNKS):
                early(k, c).wait_recv()
                late(k, c).wait_recv()

    def picked(k, b, j):
        i = picks[source[b, z * OWN + j]]
        return jnp.concatenate([chunk_of(k, c, i) for c in range(CHUNKS)], axis=0)

    def dot(a, b):
        return jnp.dot(a, b, preferred_element_type=f32)

    gram_acc[...] = jnp.zeros_like(gram_acc)
    loads[0].wait()
    for copy in loads[1:]:
        copy.start()

    for j in range(OWN):
        value = kept(j, psi[j])
        vec[0][j] = value
        put_own(0, j, value)
        gram_acc[entry(0, 0)] += pair_dot(value, value)

    pl.semaphore_wait(barrier, jnp.where(jnp.logical_and(has_prev, has_next), 5, 4))
    send_own(0)
    for copy in loads[1:3]:
        copy.wait()

    for k in range(STEPS):

        def on_site(j):
            half = dot(left[:, j].reshape(2 * blk, blk), own_block(k, j)).astype(bf16)
            both = jnp.concatenate([half[:blk], half[blk:]], axis=1)
            vec[k + 1][j] = dot(both, right[:, j].reshape(2 * blk, blk))

        exchange(k, on_site)
        if k == 0:
            for copy in loads[3:]:
                copy.wait()

        for j in range(OWN):
            both = jnp.concatenate(
                [dot(hop_left[b, j], picked(k, b, j)).astype(bf16) for b in range(HOPS)], axis=1
            )
            total = vec[k + 1][j] + dot(both, hop_right[:, j].reshape(2 * blk, blk))
            total = kept(j, total)
            vec[k + 1][j] = total
            if k + 1 < STEPS:
                put_own(k + 1, j, total)
            for i in range(k + 2):
                other = total if i == k + 1 else vec[i][j]
                gram_acc[entry(i, k + 1)] += pair_dot(total, other)
        if k + 1 < STEPS:
            send_own(k + 1)

    for e in range(len(ENTRIES)):
        line = jnp.sum(gram_acc[e], axis=0, keepdims=True)
        gram_out[e : e + 1, :] = line[:, :128] + line[:, 128:]
    gram_out[len(ENTRIES) :, :] = jnp.zeros((16 - len(ENTRIES), 128), f32)

    def gram_copy(d):
        return pltpu.make_async_remote_copy(
            src_ref=gram_out, dst_ref=gram_in.at[d - 1], send_sem=gram_send.at[d - 1],
            recv_sem=gram_recv.at[d - 1], device_id=(me_c, lax.rem(z + d, 4)), device_id_type=MESH,
        )

    for d in range(1, 4):
        gram_copy(d).start()
    for d in range(1, 4):
        gram_copy(d).wait_recv()
    gram_all = jnp.sum(gram_out[...] + gram_in[0] + gram_in[1] + gram_in[2], axis=1, keepdims=True)
    gram = [gram_all[e : e + 1] for e in range(len(ENTRIES))]

    coef = [jnp.ones((1, 1), f32)]
    for k in range(STEPS):
        h = step_size[0, k]
        self_dot = quadratic(coef, coef, gram, 0, 0)
        cross = quadratic(coef, coef, gram, 0, 1)
        grow = 1.0 + h * (cross / self_dot)
        new = [grow * c for c in coef] + [jnp.zeros((1, 1), f32)]
        for i, c in enumerate(coef):
            new[i + 1] = new[i + 1] - h * c
        scale = 1.0 / jnp.sqrt(quadratic(new, new, gram, 0, 0))
        coef = [c * scale for c in new]

    def merge(direction, j):
        src, dst, to = ((send_left, from_left, nxt), (send_right, from_right, prv))[direction]
        return pltpu.make_async_remote_copy(
            src_ref=src.at[j], dst_ref=dst.at[j], send_sem=merge_send.at[direction, j],
            recv_sem=merge_recv.at[direction, j], device_id=(to, z), device_id_type=MESH,
        )

    def finish(j, carry):
        value = coef[0] * vec[0][j]
        for i in range(1, STEPS + 1):
            value = value + coef[i] * vec[i][j]
        final[0, j] = value
        own = value.astype(bf16)
        own_t = value.T.astype(bf16)
        for a in range(2):
            half = dot(own_t, left[a, j]).astype(bf16)
            send_left[j, a] = (chi * dot(half, own)).astype(bf16)
            half = dot(right[a, j], own_t).astype(bf16)
            send_right[j, a] = (chi * dot(own, half)).astype(bf16)

        @pl.when(has_next)
        def _():
            merge(0, j).start()

        @pl.when(has_prev)
        def _():
            merge(1, j).start()

        return carry

    lax.fori_loop(0, OWN, finish, 0, unroll=True)
    def receive(direction, j, out, env, got):
        merge(direction, j).wait_recv()
        for a in range(2):
            out[0, a, j] = env[a, j].astype(f32) + got[j, a].astype(f32)

    @pl.when(has_prev)
    def _():
        for j in range(OWN):
            receive(0, j, merged_left, left, from_left)

    @pl.when(has_next)
    def _():
        for j in range(OWN):
            receive(1, j, merged_right, right, from_right)

    @pl.when(jnp.logical_not(has_prev))
    def _():
        merged_left[0] = left[...].astype(f32)

    @pl.when(jnp.logical_not(has_next))
    def _():
        merged_right[0] = right[...].astype(f32)

    for k in range(STEPS):

        @pl.when(is_outer)
        def _():
            for c in range(CHUNKS):
                to_near(k, c).wait_send()

        @pl.when(is_inner)
        def _():
            for c in range(CHUNKS):
                to_peer(k, c).wait_send()
                relay(k, c).wait_send()
                early(k, c).wait_send()
                late(k, c).wait_send()

    for d in range(1, 4):
        gram_copy(d).wait_send()

    @pl.when(has_next)
    def _():
        for j in range(OWN):
            merge(0, j).wait_send()

    @pl.when(has_prev)
    def _():
        for j in range(OWN):
            merge(1, j).wait_send()


def write_out(*refs):
    count = (len(refs) - 1) // 2
    copies = [
        pltpu.make_async_copy(refs[i].at[0, j], refs[count + i].at[0, j], refs[-1].at[i, j])
        for i in range(count)
        for j in range(refs[i].shape[1])
    ]
    for copy in copies:
        copy.start()
    for copy in copies:
        copy.wait()


def window(index, plan, psi, kept_rank, step_size, left_env, right_env, hop_left, hop_right, hop_source):
    size = SIZES[index]
    f32, bf16 = jnp.float32, jnp.bfloat16
    own, blk = psi.shape[1], psi.shape[2]
    rows = blk // CHUNKS
    env = (2, own, blk, blk)
    smem = pl.BlockSpec(memory_space=pltpu.SMEM)
    hbm = pl.BlockSpec(memory_space=pl.ANY)
    dma = pltpu.SemaphoreType.DMA
    shapes = (psi.shape, left_env.shape, right_env.shape)
    held = [pltpu.with_memory_space_constraint(x, pltpu.HBM) for x in (psi, left_env, right_env, hop_left, hop_right)]
    results = pl.pallas_call(
        functools.partial(kernel, size),
        out_shape=tuple(pltpu.VMEM(shape, f32) for shape in shapes),
        in_specs=[smem] * 4 + [hbm] * 5,
        out_specs=(pl.BlockSpec(memory_space=pltpu.VMEM),) * 3,
        scratch_shapes=[
            *[pltpu.VMEM((8, rows, blk), bf16) for _ in range(STEPS * CHUNKS)],
            *[pltpu.VMEM((OWN, rows, blk), bf16) for _ in range(2 * STEPS * CHUNKS)],
            *[
                pltpu.VMEM((CHUNKS, count, rows, blk), bf16)
                for count in (size - LATE, LATE, size - LATE, LATE)
                for _ in range(STEPS)
            ],
            *[pltpu.VMEM((own, blk, blk), f32) for _ in range(STEPS + 1)],
            pltpu.VMEM((own, blk, blk), f32),
            *[pltpu.VMEM(env, bf16) for _ in range(4)],
            *[pltpu.VMEM((own, 2, blk, blk), bf16) for _ in range(4)],
            pltpu.VMEM((len(ENTRIES), 8, blk), f32),
            pltpu.VMEM((3, 16, 128), f32),
            pltpu.VMEM((16, 128), f32),
            pltpu.SMEM((32,), jnp.int32),
            dma((5,)),
            dma((STEPS, CHUNKS, 4)),
            dma((STEPS, CHUNKS, 3)),
            dma((3,)),
            dma((3,)),
            dma((2, own)),
            dma((2, own)),
        ],
        compiler_params=pltpu.CompilerParams(
            collective_id=index, has_side_effects=True, vmem_limit_bytes=61_700_000
        ),
    )(kept_rank, step_size, hop_source, plan, *held)
    return pl.pallas_call(
        write_out,
        out_shape=tuple(jax.ShapeDtypeStruct(shape, f32) for shape in shapes),
        in_specs=[pl.BlockSpec(memory_space=pltpu.VMEM)] * 3,
        out_specs=(hbm,) * 3,
        scratch_shapes=[dma((3, own))],
        compiler_params=pltpu.CompilerParams(vmem_limit_bytes=8 * 1024 * 1024),
    )(*[pltpu.with_memory_space_constraint(x, pltpu.VMEM) for x in results])


def on_device(*args):
    smem = pl.BlockSpec(memory_space=pltpu.SMEM)
    plan, choice = pl.pallas_call(
        plan_kernel,
        out_shape=(jax.ShapeDtypeStruct((4,), jnp.int32), jax.ShapeDtypeStruct((1,), jnp.int32)),
        in_specs=[smem],
        out_specs=(smem, smem),
    )(args[-1])
    return lax.switch(choice.reshape(()), [functools.partial(window, i) for i in range(len(SIZES))], plan, *args)


def solution(mesh):
    part = P("chain", "sector", None, None)
    term = P("chain", None, "sector", None, None)
    return jax.shard_map(
        on_device,
        mesh=mesh,
        in_specs=(part, P("chain", "sector"), P("chain", None), term, term, term, term, P()),
        out_specs=(part, term, term),
        check_vma=False,
    )
```
